32 devices in a mesh: fsdp: 4 (over y, x), context: 4 (over z), tensor: 2 (over core).
Axes of the slice: x: 2, y: 2, z: 4, core: 2. Of those that a mesh axis runs over, the one named last changes fastest.
Arguments:
- tokens: bfloat16 [4096, 1024], P(('fsdp', 'context')), may hold values from -6 to 6
- lengths: int32 [4, 4], P('fsdp'), may hold values from 1 to 896, 1024 in all within a row
- deal: int32 [4, 1024], P('fsdp', 'context'), may hold values from 0 to 1023, as said below
- attn_norm_gain: float32 [1024], replicated, may hold values from 0.5 to 1.5
- ff_norm_gain: float32 [1024], replicated, may hold values from 0.5 to 1.5
- w_query: bfloat16 [1024, 512], P('fsdp', 'tensor'), may hold values from -0.1875 to 0.1875
- w_key: bfloat16 [1024, 128], P('fsdp', 'tensor'), may hold values from -0.1875 to 0.1875
- w_value: bfloat16 [1024, 128], P('fsdp', 'tensor'), may hold values from -0.1875 to 0.1875
- w_attn_out: bfloat16 [1024, 512], P('fsdp', 'tensor'), may hold values from -2 to 2
- w_gate_z: bfloat16 [1024, 1536], P('fsdp', 'tensor'), may hold values from -0.1875 to 0.1875
- w_ssm_in: bfloat16 [1024, 1536], P('fsdp', 'tensor'), may hold values from -0.1875 to 0.1875
- w_bc: bfloat16 [1024, 256], P('fsdp'), may hold values from -0.1875 to 0.1875
- w_step: bfloat16 [1024, 24], P('fsdp', 'tensor'), may hold values from -0.1875 to 0.1875
- w_ssm_out: bfloat16 [1024, 1536], P('fsdp', 'tensor'), may hold values from -0.15625 to 0.15625
- conv_ssm: float32 [1536, 4], P('tensor'), may hold values from -3 to 3
- conv_bc: float32 [256, 4], replicated, may hold values from -3 to 3
- step_bias: float32 [24], P('tensor'), may hold values from -2 to 1
- decay_log: float32 [24], P('tensor'), may hold values from -8 to 0
- skip_gain: float32 [24], P('tensor'), may hold values from 0.5 to 1.5
- ssm_norm_gain: float32 [1536], P('tensor'), may hold values from 0.5 to 1.5
- w_gate: bfloat16 [1024, 2048], P('fsdp', 'tensor'), may hold values from -0.1875 to 0.1875
- w_up: bfloat16 [1024, 2048], P('fsdp', 'tensor'), may hold values from -0.1875 to 0.1875
- w_down: bfloat16 [1024, 2048], P('fsdp', 'tensor'), may hold values from -0.125 to 0.125
- cotangent: bfloat16 [4096, 1024], P(('fsdp', 'context')), may hold values from -6 to 6
Outputs:
- output: bfloat16 [4096, 1024], P(('fsdp', 'context'))
- input_grad: float32 [4096, 1024], P(('fsdp', 'context'))
- grad_attn_norm_gain: float32 [1024], replicated
- grad_ff_norm_gain: float32 [1024], replicated
- grad_w_query: float32 [1024, 512], P('fsdp', 'tensor')
- grad_w_key: float32 [1024, 128], P('fsdp', 'tensor')
- grad_w_value: float32 [1024, 128], P('fsdp', 'tensor')
- grad_w_attn_out: float32 [1024, 512], P('fsdp', 'tensor')
- grad_w_gate_z: float32 [1024, 1536], P('fsdp', 'tensor')
- grad_w_ssm_in: float32 [1024, 1536], P('fsdp', 'tensor')
- grad_w_bc: float32 [1024, 256], P('fsdp')
- grad_w_step: float32 [1024, 24], P('fsdp', 'tensor')
- grad_w_ssm_out: float32 [1024, 1536], P('fsdp', 'tensor')
- grad_conv_ssm: float32 [1536, 4], P('tensor')
- grad_conv_bc: float32 [256, 4], replicated
- grad_step_bias: float32 [24], P('tensor')
- grad_decay_log: float32 [24], P('tensor')
- grad_skip_gain: float32 [24], P('tensor')
- grad_ssm_norm_gain: float32 [1536], P('tensor')
- grad_w_gate: float32 [1024, 2048], P('fsdp', 'tensor')
- grad_w_up: float32 [1024, 2048], P('fsdp', 'tensor')
- grad_w_down: float32 [1024, 2048], P('fsdp', 'tensor')
- rms_stats: float32 [3], replicated
The draws below stay inside these ranges and needn't reach their ends.
Inputs may be any that keep to these rules, and one draw needn't show every extreme that they name: Row g lists in order the lengths of the 4 sequences packed into token group g; each row sums to 1024 and its largest entry is 896. With P = 256 / 4 and one shift s of 0 to 4 - 1 for each group, row d * 256 + j * P + i of group g (j < 4, i < P) holds place j * 256 + ((d + s) mod 4) * P + i; each row of deal is a permutation of the group's places.
All inputs are finite; a program needn't handle non-finite values.
Results may differ from the reference program's by a relative error of at most 0.019.
Values may be sent and summed in bfloat16 or wider, within the bound.
A program may use at most 192 MiB of HBM per device.

```python
import math
import jax
import jax.numpy as jnp
import numpy as np
from jax import lax

D = 1024
QUERY_HEADS = 8
KEY_VALUE_HEADS = 2
HEAD_WIDTH = 64
SPACE_HEADS = 24
SPACE_HEAD_WIDTH = 64
STATE_WIDTH = 128
KC = 4
FF = 2048
TOK_DEV = 256
SEQS = 4
GROUP = 1024
MAX_LEN = 896
TOKENS = 4096
DQ = 512
DKV = 128
DI = 1536
N_FSDP = 4
N_CONTEXT = 4


def draw_deal(key, part):
    shifts = jax.random.randint(jax.random.fold_in(key, 17), (N_FSDP, 1), 0, N_CONTEXT).astype(jnp.int32)
    piece_rows = TOK_DEV // N_CONTEXT
    rows = jnp.arange(GROUP, dtype=jnp.int32)[None, :]
    device = rows // TOK_DEV
    within = rows % TOK_DEV
    slot = within // piece_rows
    inner_width = within % piece_rows
    return (slot * TOK_DEV + (device + shifts) % N_CONTEXT * piece_rows + inner_width).astype(jnp.int32)


def block_levels(own_key, dims, cuts, least, top_value):
    level, own = 1.0, jax.random.fold_in(own_key, 6)
    for axis_at, shards_of in cuts:
        draws = jnp.exp(jax.random.uniform(jax.random.fold_in(own, axis_at), (shards_of,), jnp.float32, least / len(cuts), top_value / len(cuts)))
        level = level * jnp.repeat(draws, dims[axis_at] // shards_of).reshape([-1 if axis == axis_at else 1 for axis in range(len(dims))])
    return level


def split_up(number_of, total, limit, skew):
    weights = [(1 << 20) // math.isqrt(rank ** skew) + 1 for rank in range(2, number_of + 1)]
    spare, counts = total - limit - (number_of - 1), [1] * (number_of - 1)
    while spare > 0:
        candidates = [i for i in range(number_of - 1) if counts[i] < limit]
        pool, budget = sum([weights[i] for i in candidates]), spare
        for i in candidates:
            addition = min(limit - counts[i], max(1, budget * weights[i] // pool), spare)
            counts[i] = counts[i] + addition
            spare = spare - addition
    return np.array([limit] + counts)


def uneven(key, count, total, limit, skew):
    if count == 2:
        one = jax.random.randint(key, (), max(1, total - limit), min(limit, total - 1) + 1)
        return jnp.stack([one, total - one])
    sizes = jnp.asarray(split_up(count, total, limit, skew), jnp.int32)
    twos = (count - 1) // 2
    source_of, sink = sizes[1:1 + 2 * twos:2], sizes[2:2 + 2 * twos:2]
    room = jnp.minimum(source_of - 1, limit - sink)
    passed = jax.random.randint(jax.random.fold_in(key, 1), (twos,), 0, 1 << 20) % (room + 1)
    sizes = sizes.at[1:1 + 2 * twos:2].set(source_of - passed).at[2:2 + 2 * twos:2].set(sink + passed)
    return sizes[jax.random.permutation(jax.random.fold_in(key, 2), count)]


def bell_draw(stream_key, extent, scale, reach, split=(), kind=jnp.bfloat16):
    values = scale * jax.random.normal(stream_key, extent, jnp.float32)
    if split:
        values = values * block_levels(stream_key, extent, split, -0.22, 0.18)
    return jnp.clip(values, -reach, reach).astype(kind)


def setup_inputs(seed: int = 0) -> dict:
    splits = jax.random.split(jax.random.key(seed), 25)
    tokens = bell_draw(splits[0], (TOKENS, D), 1.0, 6.0, ((0, 16),))
    lengths = jax.vmap(lambda own: uneven(own, SEQS, GROUP, MAX_LEN, 1))(jax.random.split(splits[1], N_FSDP)).reshape((N_FSDP, SEQS)).astype(jnp.int32)
    deal = draw_deal(jax.random.fold_in(splits[24], 71), 0)
    attn_norm_gain = jnp.clip(1.0 + 0.1 * jax.random.normal(splits[3], (D,), jnp.float32), 0.5, 1.5)
    ff_norm_gain = jnp.clip(1.0 + 0.1 * jax.random.normal(splits[4], (D,), jnp.float32), 0.5, 1.5)
    w_query = bell_draw(splits[5], (D, DQ), D ** -0.5, 0.1875, ((0, 4), (1, 2)))
    w_key = bell_draw(splits[6], (D, DKV), D ** -0.5, 0.1875, ((0, 4), (1, 2)))
    w_value = bell_draw(splits[7], (D, DKV), D ** -0.5, 0.1875, ((0, 4), (1, 2)))
    w_attn_out = bell_draw(splits[8], (D, DQ), (max(1, DQ * 16 // MAX_LEN)) ** -0.5, 2.0, ((0, 4), (1, 2)))
    w_gate_z = bell_draw(splits[9], (D, DI), D ** -0.5, 0.1875, ((0, 4), (1, 2)))
    w_ssm_in = bell_draw(splits[10], (D, DI), D ** -0.5, 0.1875, ((0, 4), (1, 2)))
    w_bc = bell_draw(splits[11], (D, 2 * STATE_WIDTH), D ** -0.5, 0.1875, ((0, 4),))
    w_step = bell_draw(splits[12], (D, SPACE_HEADS), D ** -0.5, 0.1875, ((0, 4), (1, 2)))
    w_ssm_out = bell_draw(splits[13], (D, DI), DI ** -0.5, 0.15625, ((0, 4), (1, 2)))
    conv_ssm = bell_draw(splits[14], (DI, KC), KC ** -0.5, 3.0, ((0, 2),), jnp.float32)
    conv_bc = bell_draw(splits[15], (2 * STATE_WIDTH, KC), KC ** -0.5, 3.0, (), jnp.float32)
    step_bias = jnp.clip(-2.0 + 3.0 * jax.random.uniform(splits[16], (SPACE_HEADS,), jnp.float32) ** block_levels(splits[16], (SPACE_HEADS,), ((0, 2),), -0.2, 0.2), -2.0, 1.0)
    decay_log = jnp.clip(-8.0 + 8.0 * jax.random.uniform(splits[17], (SPACE_HEADS,), jnp.float32) ** block_levels(splits[17], (SPACE_HEADS,), ((0, 2),), -0.2, 0.2), -8.0, 0.0)
    skip_gain = jnp.clip(0.5 + 1.0 * jax.random.uniform(splits[18], (SPACE_HEADS,), jnp.float32) ** block_levels(splits[18], (SPACE_HEADS,), ((0, 2),), -0.2, 0.2), 0.5, 1.5)
    ssm_norm_gain = jnp.clip(1.0 + 0.1 * jax.random.normal(splits[19], (DI,), jnp.float32), 0.5, 1.5)
    w_gate = bell_draw(splits[20], (D, FF), D ** -0.5, 0.1875, ((0, 4), (1, 2)))
    w_up = bell_draw(splits[21], (D, FF), D ** -0.5, 0.1875, ((0, 4), (1, 2)))
    w_down = bell_draw(splits[22], (D, FF), FF ** -0.5, 0.125, ((0, 4), (1, 2)))
    cotangent = bell_draw(splits[23], (TOKENS, D), 1.0, 6.0, ((0, 16),))
    return {"tokens": tokens, "lengths": lengths, "deal": deal, "attn_norm_gain": attn_norm_gain, "ff_norm_gain": ff_norm_gain, "w_query": w_query, "w_key": w_key, "w_value": w_value, "w_attn_out": w_attn_out, "w_gate_z": w_gate_z, "w_ssm_in": w_ssm_in, "w_bc": w_bc, "w_step": w_step, "w_ssm_out": w_ssm_out, "conv_ssm": conv_ssm, "conv_bc": conv_bc, "step_bias": step_bias, "decay_log": decay_log, "skip_gain": skip_gain, "ssm_norm_gain": ssm_norm_gain, "w_gate": w_gate, "w_up": w_up, "w_down": w_down, "cotangent": cotangent}


@jax.custom_vjp
def lower_precision(v):
    return lax.optimization_barrier(v.astype(jnp.bfloat16)).astype(jnp.float32)

@jax.custom_vjp
def low_back(v):
    return v

def low_keep(v):
    return (lower_precision(v), None)

def low_pass(kept, grad):
    return (grad,)

def back_keep(v):
    return (v, None)

def back_low(kept, grad):
    return (lower_precision(grad),)
lower_precision.defvjp(low_keep, low_pass)
low_back.defvjp(back_keep, back_low)
epsilon = 1e-06
rope_base = 100000000000.0
masked_value = -1e+30
highest = lax.Precision.HIGHEST

def matmul(left, right):
    return jnp.dot(left, right, precision=highest, preferred_element_type=jnp.float32)

def segments_of(lengths_row, positions):
    ends = jnp.cumsum(lengths_row).astype(jnp.int32)
    seg_ids = lax.optimization_barrier(jnp.sum((positions[:, None] >= ends[None, :]).astype(jnp.int32), axis=1)).astype(jnp.int32)
    starts = lax.optimization_barrier(jnp.max(jnp.where(ends[None, :] <= positions[:, None], ends[None, :], 0), axis=1)).astype(jnp.int32)
    return (seg_ids, starts)

def apply_rotary(value_matrix, sequence_position, head_list, sign):
    half_width = value_matrix.shape[-1] // (2 * head_list)
    freqs = rope_base ** (-jnp.arange(half_width, dtype=jnp.float32) / half_width)
    angles = sequence_position.astype(jnp.float32)[:, None] * freqs[None, :]
    cosine = jnp.cos(angles)[:, None, :]
    sine_part = sign * jnp.sin(angles)[:, None, :]
    shaped = value_matrix.reshape(value_matrix.shape[0], head_list, 2 * half_width)
    first_part = shaped[..., :half_width]
    second_part = shaped[..., half_width:]
    turned = jnp.concatenate([first_part * cosine - second_part * sine_part, second_part * cosine + first_part * sine_part], axis=-1)
    return turned.reshape(value_matrix.shape)

def rms_scale(value_matrix):
    return value_matrix * lax.rsqrt(lax.optimization_barrier(jnp.mean(value_matrix * value_matrix, axis=-1, keepdims=True)) + epsilon)

def causal_conv(extended, conv_weight, seg_extended, segment_rows):
    count_of_rows = segment_rows.shape[0]
    summed = jnp.zeros((count_of_rows, extended.shape[1]), jnp.float32)
    for offset in range(conv_weight.shape[1]):
        window = extended[offset:offset + count_of_rows]
        keep_mask = (seg_extended[offset:offset + count_of_rows] == segment_rows).astype(jnp.float32)
        summed = summed + window * keep_mask[:, None] * conv_weight[:, offset][None, :]
    return jax.nn.silu(summed)

def ssd_local(scan_inputs, input_matrix, output_matrix, step_size, rate, skip_gain, segment_rows, segment_before):
    count_of_rows = segment_rows.shape[0]
    log_decay = step_size * rate[None, :]
    cumulative = jnp.cumsum(log_decay, axis=0)
    order = jnp.arange(count_of_rows, dtype=jnp.int32)
    joined = (segment_rows[:, None] == segment_rows[None, :]) & (order[:, None] >= order[None, :])
    differ = cumulative.T[:, :, None] - cumulative.T[:, None, :]
    within = jnp.exp(jnp.where(joined[None], differ, masked_value))
    intersection = jnp.dot(output_matrix, input_matrix.T, precision=highest, preferred_element_type=jnp.float32)
    scaled = scan_inputs * step_size[:, :, None]
    local_out = jnp.einsum('hts,shp->thp', within * intersection[None], scaled, precision=highest)
    fresh = (segment_rows == segment_before).astype(jnp.float32)
    carry_gain = fresh[:, None] * jnp.exp(cumulative)
    tail = (segment_rows == segment_rows[count_of_rows - 1]).astype(jnp.float32)[:, None] * jnp.exp(cumulative[count_of_rows - 1][None, :] - cumulative)
    fresh_state = jnp.einsum('sh,shp,sn->hpn', tail, scaled, input_matrix, precision=highest)
    whole_decay = carry_gain[count_of_rows - 1]
    local_out = local_out + skip_gain[None, :, None] * scan_inputs
    return (local_out, carry_gain, whole_decay, fresh_state)

def attention(query_full_rows, key_full_rows, value_full_rows, positions, starts):
    group_row_list = query_full_rows.shape[0]
    block_row_list = min(512, group_row_list)
    query_per_group = QUERY_HEADS // KEY_VALUE_HEADS
    key_matrix = key_full_rows.reshape(group_row_list, KEY_VALUE_HEADS, HEAD_WIDTH)
    value_matrix = value_full_rows.reshape(group_row_list, KEY_VALUE_HEADS, HEAD_WIDTH)

    def one_block(block_index):
        block_first_row = block_index * block_row_list
        query_matrix = lax.dynamic_slice_in_dim(query_full_rows, block_first_row, block_row_list, 0).reshape(block_row_list, KEY_VALUE_HEADS, query_per_group, HEAD_WIDTH)
        query_pos = lax.dynamic_slice_in_dim(positions, block_first_row, block_row_list, 0)
        query_start = lax.dynamic_slice_in_dim(starts, block_first_row, block_row_list, 0)
        raw_scores = jnp.einsum('qgjd,kgd->gjqk', query_matrix, key_matrix, precision=highest) * HEAD_WIDTH ** (-0.5)
        scores = low_back(raw_scores)
        allowed = (positions[None, :] <= query_pos[:, None]) & (positions[None, :] >= query_start[:, None])
        masked = jnp.where(allowed[None, None], scores, masked_value)
        peak_value = lax.optimization_barrier(jnp.max(masked, axis=-1, keepdims=True))
        weights = jnp.exp(masked - peak_value)
        prob_values = weights / lax.optimization_barrier(jnp.sum(weights, axis=-1, keepdims=True))
        mixed = jnp.einsum('gjqk,kgd->qgjd', lower_precision(prob_values), value_matrix, precision=highest)
        return mixed.reshape(block_row_list, QUERY_HEADS * HEAD_WIDTH)
    blocks = lax.map(jax.checkpoint(one_block), jnp.arange(group_row_list // block_row_list, dtype=jnp.int32))
    return blocks.reshape(group_row_list, QUERY_HEADS * HEAD_WIDTH)

def layer(tokens_f, params, lengths_row):
    attn_norm_gain, ff_norm_gain, w_query, w_key, w_value, w_attn_out, w_gate_z, w_ssm_in, w_bc, w_step, w_ssm_out, conv_ssm, conv_bc, step_bias, decay_log, skip_gain, ssm_norm_gain, w_gate, w_up, w_down = params
    group_row_list = tokens_f.shape[0]
    positions = jnp.arange(group_row_list, dtype=jnp.int32)
    segment_rows, starts = segments_of(lengths_row, positions)
    sequence_position = positions - starts
    normed = lower_precision(rms_scale(tokens_f) * attn_norm_gain)
    query_pre = low_back(matmul(normed, w_query))
    key_before_rotary = low_back(matmul(normed, w_key))
    value_full_rows = lower_precision(low_back(matmul(normed, w_value)))
    query_full_rows = lower_precision(apply_rotary(query_pre, sequence_position, QUERY_HEADS, 1.0))
    key_full_rows = lower_precision(apply_rotary(key_before_rotary, sequence_position, KEY_VALUE_HEADS, 1.0))
    attended = lower_precision(low_back(attention(query_full_rows, key_full_rows, value_full_rows, positions, starts)))
    attn_part = matmul(attended, w_attn_out.T)
    gate_z = low_back(matmul(normed, w_gate_z))
    conv_in = lower_precision(low_back(matmul(normed, jnp.concatenate([w_ssm_in, w_bc], axis=1))))
    step_raw = low_back(matmul(normed, w_step))
    extended = jnp.concatenate([jnp.zeros((KC - 1, conv_in.shape[1]), jnp.float32), conv_in], axis=0)
    seg_extended = jnp.concatenate([jnp.full((KC - 1,), -1, jnp.int32), segment_rows])
    active_rows = causal_conv(extended, jnp.concatenate([conv_ssm, conv_bc], axis=0), seg_extended, segment_rows)
    inner_width = SPACE_HEADS * SPACE_HEAD_WIDTH
    scan_inputs = active_rows[:, :inner_width].reshape(group_row_list, SPACE_HEADS, SPACE_HEAD_WIDTH)
    input_matrix = active_rows[:, inner_width:inner_width + STATE_WIDTH]
    output_matrix = active_rows[:, inner_width + STATE_WIDTH:]
    step_size = jax.nn.softplus(step_raw + step_bias[None, :])
    rate = -jnp.exp(decay_log)
    stretch_rows = TOK_DEV
    stretch_list = group_row_list // stretch_rows
    segment_before = jnp.concatenate([jnp.full((1,), -1, jnp.int32), segment_rows[stretch_rows - 1:group_row_list - 1:stretch_rows]])

    def stretch_step(state_in, pieces):
        piece_u, piece_b, piece_c, piece_step, piece_seg, piece_before = pieces
        local_out, carry_gain, whole_decay, fresh_state = ssd_local(piece_u, piece_b, piece_c, piece_step, rate, skip_gain, piece_seg, piece_before)
        carried = jnp.einsum('hpn,tn->thp', state_in, piece_c, precision=highest)
        result = local_out + carry_gain[:, :, None] * carried
        return (whole_decay[:, None, None] * state_in + fresh_state, result)
    stretch_inputs = (scan_inputs.reshape(stretch_list, stretch_rows, SPACE_HEADS, SPACE_HEAD_WIDTH), input_matrix.reshape(stretch_list, stretch_rows, STATE_WIDTH), output_matrix.reshape(stretch_list, stretch_rows, STATE_WIDTH), step_size.reshape(stretch_list, stretch_rows, SPACE_HEADS), segment_rows.reshape(stretch_list, stretch_rows), segment_before)
    closing_state, space_output = lax.scan(jax.checkpoint(stretch_step), jnp.zeros((SPACE_HEADS, SPACE_HEAD_WIDTH, STATE_WIDTH), jnp.float32), stretch_inputs)
    ssm_y = space_output.reshape(group_row_list, inner_width)
    gated = ssm_y * jax.nn.silu(gate_z)
    mixed = lower_precision(rms_scale(gated) * ssm_norm_gain)
    ssm_part = matmul(mixed, w_ssm_out.T)
    mixer = low_back(attn_part + ssm_part)
    resid = tokens_f + mixer
    normed_ff = lower_precision(rms_scale(resid) * ff_norm_gain)
    gate_v = low_back(matmul(normed_ff, w_gate))
    up_v = low_back(matmul(normed_ff, w_up))
    hidden = lower_precision(jax.nn.silu(gate_v) * up_v)
    ff_part = low_back(matmul(hidden, w_down.T))
    final = resid + ff_part
    sums = jnp.stack([jnp.sum(final * final), jnp.sum(mixer * mixer), jnp.sum(ff_part * ff_part)])
    return (final, sums)

def reference(tokens, lengths, deal, attn_norm_gain, ff_norm_gain, w_query, w_key, w_value, w_attn_out, w_gate_z, w_ssm_in, w_bc, w_step, w_ssm_out, conv_ssm, conv_bc, step_bias, decay_log, skip_gain, ssm_norm_gain, w_gate, w_up, w_down, cotangent):
    params = tuple((item.astype(jnp.float32) for item in (attn_norm_gain, ff_norm_gain, w_query, w_key, w_value, w_attn_out, w_gate_z, w_ssm_in, w_bc, w_step, w_ssm_out, conv_ssm, conv_bc, step_bias, decay_log, skip_gain, ssm_norm_gain, w_gate, w_up, w_down)))
    tok_groups = tokens.astype(jnp.float32).reshape(N_FSDP, GROUP, D)
    cot_groups = cotangent.astype(jnp.float32).reshape(N_FSDP, GROUP, D)

    def one_group(totals, pieces):
        dealt_tokens, dealt_cot, lengths_row, deal_row = pieces
        place_index = deal_row.astype(jnp.int32)
        group_tokens = jnp.zeros_like(dealt_tokens).at[place_index].set(dealt_tokens)
        group_cot = jnp.zeros_like(dealt_cot).at[place_index].set(dealt_cot)

        def forward(group_in, weights):
            return layer(group_in, weights, lengths_row)
        final, pullback, sums = jax.vjp(forward, group_tokens, params, has_aux=True)
        grad_in, grad_weights = pullback(group_cot)
        grad_totals, stat_totals = totals
        updated = jax.tree.map(lambda left, right: left + right, grad_totals, grad_weights)
        return ((updated, stat_totals + sums), (final.astype(jnp.bfloat16), grad_in))
    start_totals = (jax.tree.map(jnp.zeros_like, params), jnp.zeros((3,), jnp.float32))
    (grad_totals, stat_totals), (finals, grads_in) = lax.scan(one_group, start_totals, (tok_groups, cot_groups, lengths, deal))
    rms_stats = jnp.sqrt(stat_totals / (TOKENS * D))
    return (finals.reshape(TOKENS, D), grads_in.reshape(TOKENS, D)) + tuple(grad_totals) + (rms_stats,)
```

```python
import jax
import jax.numpy as jnp
from jax import lax
from jax.sharding import PartitionSpec as P

D = 1024
QUERY_HEADS = 8
HEAD_WIDTH = 64
SPACE_HEADS = 24
SPACE_HEAD_WIDTH = 64
STATE_WIDTH = 128
KC = 4
DI = 1536


epsilon = 1e-06
rope_base = 100000000000.0
masked_value = -1e30
highest = lax.Precision.HIGHEST


def passed_along(block, axis, distance):
    devices = range(lax.axis_size(axis))
    route = [(i - distance, i) for i in devices if i - distance in devices]
    return lax.ppermute(block, axis, route)


def matmul_low(left, right):
    return jnp.dot(left, right, preferred_element_type=jnp.float32)


def matmul_tn(left, right):
    return lax.dot_general(
        left, right, (((0,), (0,)), ((), ())), preferred_element_type=jnp.float32
    )


def matmul_nt(left, right):
    return lax.dot_general(
        left, right, (((1,), (1,)), ((), ())), preferred_element_type=jnp.float32
    )


def segments_of(lengths_row, positions):
    ends = jnp.cumsum(lengths_row)
    seg_ids = jnp.sum((positions[:, None] >= ends[None, :]).astype(jnp.int32), axis=1)
    starts = jnp.max(jnp.where(ends[None, :] <= positions[:, None], ends[None, :], 0), axis=1)
    return (seg_ids, starts)


def apply_rotary(value_matrix, sequence_position, head_list, sign):
    half_width = value_matrix.shape[-1] // (2 * head_list)
    freqs = rope_base ** (-jnp.arange(half_width, dtype=jnp.float32) / half_width)
    angles = sequence_position.astype(jnp.float32)[:, None] * freqs[None, :]
    cosine = jnp.cos(angles)[:, None, :]
    sine_part = sign * jnp.sin(angles)[:, None, :]
    shaped = value_matrix.reshape(value_matrix.shape[0], head_list, 2 * half_width)
    first_part = shaped[..., :half_width]
    second_part = shaped[..., half_width:]
    turned = jnp.concatenate(
        [
            first_part * cosine - second_part * sine_part,
            second_part * cosine + first_part * sine_part,
        ],
        axis=-1,
    )
    return turned.reshape(value_matrix.shape)


def causal_conv(extended, conv_weight, seg_extended, segment_rows):
    count_of_rows = segment_rows.shape[0]
    summed = jnp.zeros((count_of_rows, extended.shape[1]), jnp.float32)
    for offset in range(conv_weight.shape[1]):
        window = extended[offset : offset + count_of_rows]
        keep_mask = (seg_extended[offset : offset + count_of_rows] == segment_rows).astype(
            jnp.float32
        )
        summed = summed + window * keep_mask[:, None] * conv_weight[:, offset][None, :]
    return jax.nn.silu(summed)


def ssd_local(
    scan_inputs,
    input_matrix,
    output_matrix,
    step_size,
    rate,
    skip_gain,
    segment_rows,
    segment_before,
):
    count_of_rows = segment_rows.shape[0]
    log_decay = step_size * rate[None, :]
    cumulative = jnp.cumsum(log_decay, axis=0)
    order = jnp.arange(count_of_rows, dtype=jnp.int32)
    joined = (segment_rows[:, None] == segment_rows[None, :]) & (order[:, None] >= order[None, :])
    differ = cumulative.T[:, :, None] - cumulative.T[:, None, :]
    within = jnp.exp(jnp.where(joined[None], differ, masked_value))
    intersection = jnp.dot(
        output_matrix, input_matrix.T, precision=highest, preferred_element_type=jnp.float32
    )
    scaled = scan_inputs * step_size[:, :, None]
    local_out = jnp.einsum("hts,shp->thp", within * intersection[None], scaled, precision=highest)
    fresh = (segment_rows == segment_before).astype(jnp.float32)
    carry_gain = fresh[:, None] * jnp.exp(cumulative)
    tail = (segment_rows == segment_rows[count_of_rows - 1]).astype(jnp.float32)[:, None] * jnp.exp(
        cumulative[count_of_rows - 1][None, :] - cumulative
    )
    fresh_state = jnp.einsum("sh,shp,sn->hpn", tail, scaled, input_matrix, precision=highest)
    whole_decay = carry_gain[count_of_rows - 1]
    local_out = local_out + skip_gain[None, :, None] * scan_inputs
    return (local_out, carry_gain, whole_decay, fresh_state)


def mixer_local(
    extended,
    conv_weight,
    step_raw,
    step_bias,
    decay_log,
    skip_gain,
    seg_extended,
    segment_rows,
    segment_before,
    head_list,
):
    active_rows = causal_conv(extended, conv_weight, seg_extended, segment_rows)
    inner_width = head_list * SPACE_HEAD_WIDTH
    scan_inputs = active_rows[:, :inner_width].reshape(
        active_rows.shape[0], head_list, SPACE_HEAD_WIDTH
    )
    input_matrix = active_rows[:, inner_width : inner_width + STATE_WIDTH]
    output_matrix = active_rows[:, inner_width + STATE_WIDTH :]
    step_size = jax.nn.softplus(step_raw + step_bias[None, :])
    rate = -jnp.exp(decay_log)
    local_out, carry_gain, whole_decay, fresh_state = ssd_local(
        scan_inputs,
        input_matrix,
        output_matrix,
        step_size,
        rate,
        skip_gain,
        segment_rows,
        segment_before,
    )
    return (local_out, carry_gain, output_matrix, whole_decay, fresh_state)


def swap(block, axis, bit):
    route = [(i, i ^ bit) for i in range(lax.axis_size(axis))]
    return lax.ppermute(block, axis, route)


def over_tensor(block):
    return block + swap(block, "tensor", 1)


def relative(block, shard, axis):
    width = D // 4
    parts = [lax.slice_in_dim(block, k * width, (k + 1) * width, axis=axis) for k in range(4)]
    odd = (shard & 1) == 1
    parts = [jnp.where(odd, parts[k ^ 1], parts[k]) for k in range(4)]
    high = (shard >> 1) == 1
    parts = [jnp.where(high, parts[k ^ 2], parts[k]) for k in range(4)]
    return jnp.concatenate(parts, axis=axis)


def gather_shards(own):
    half = own.shape[0] // 2
    from_x = swap(own, "fsdp", 1)
    from_y = swap(own, "fsdp", 2)
    top = swap(from_x[:half], "fsdp", 2)
    low = swap(from_y[half:], "fsdp", 1)
    return jnp.concatenate([own, from_x, from_y, top, low], axis=0)


def scatter_sum(blocks):
    rows = blocks.shape[0] // 4
    half = rows // 2
    top = swap(blocks[3 * rows : 3 * rows + half], "fsdp", 2)
    low = swap(blocks[3 * rows + half :], "fsdp", 1)
    to_x = jnp.concatenate([plus(blocks[rows : rows + half], top), blocks[rows + half : 2 * rows]])
    to_y = jnp.concatenate(
        [blocks[2 * rows : 2 * rows + half], plus(blocks[2 * rows + half : 3 * rows], low)]
    )
    from_x = swap(to_x, "fsdp", 1)
    from_y = swap(to_y, "fsdp", 2)
    total = (
        blocks[:rows].astype(jnp.float32)
        + from_x.astype(jnp.float32)
        + from_y.astype(jnp.float32)
    )
    return total.astype(jnp.bfloat16)


def plus(left, right):
    return (left.astype(jnp.float32) + right.astype(jnp.float32)).astype(jnp.bfloat16)


def sum_context(block):
    index = lax.axis_index("context")
    bits = []
    bit = 1
    while bit < lax.axis_size("context"):
        bits.append(bit)
        half = block.shape[0] // 2
        upper = (index & bit) != 0
        low, top = block[:half], block[half:]
        kept = jnp.where(upper, top, low)
        sent = jnp.where(upper, low, top)
        block = plus(kept, swap(sent, "context", bit))
        bit *= 2
    for bit in reversed(bits):
        upper = (index & bit) != 0
        other = swap(block, "context", bit)
        block = jnp.concatenate(
            [jnp.where(upper, other, block), jnp.where(upper, block, other)], axis=0
        )
    return block


def sum_small(vector):
    for axis in ("fsdp", "context"):
        bit = 1
        while bit < lax.axis_size(axis):
            vector = vector + swap(vector, axis, bit)
            bit *= 2
    return vector


def deal_rows(block, shift):
    contexts = lax.axis_size("context")
    pieces = block.reshape(contexts, block.shape[0] // contexts, block.shape[1])
    if contexts > 4:
        dealt = lax.all_to_all(pieces, "context", split_axis=0, concat_axis=0, tiled=True)
        return jnp.roll(dealt, shift, axis=0).reshape(block.shape)
    index = lax.axis_index("context")
    got = []
    for k in range(contexts):
        piece = lax.dynamic_index_in_dim(pieces, index ^ k, 0, keepdims=False)
        got.append(swap(piece, "context", k) if k else piece)
    ordered = []
    for q in range(contexts):
        from_index = jnp.mod(q - shift, contexts) ^ index
        chosen = got[0]
        for k in range(1, contexts):
            chosen = jnp.where(from_index == k, got[k], chosen)
        ordered.append(chosen)
    return jnp.concatenate(ordered, axis=0)


def gather_earlier(block):
    contexts = lax.axis_size("context")
    if contexts > 4:
        return lax.all_gather(block, "context", axis=0)
    index = lax.axis_index("context")
    got = [block] + [passed_along(block, "context", k) for k in range(1, contexts)]
    ordered = []
    for j in range(contexts):
        chosen = block
        for k in range(1, contexts):
            chosen = jnp.where(index - j == k, got[k], chosen)
        ordered.append(chosen)
    return jnp.stack(ordered)


def scatter_earlier(blocks):
    contexts = lax.axis_size("context")
    if contexts > 4:
        return lax.psum_scatter(
            blocks.astype(jnp.bfloat16), "context", scatter_dimension=0, tiled=False
        ).astype(jnp.float32)
    index = lax.axis_index("context")
    total = lax.dynamic_index_in_dim(blocks, index, 0, keepdims=False)
    low = blocks.astype(jnp.bfloat16)
    for k in range(1, contexts):
        sent = lax.dynamic_index_in_dim(low, jnp.maximum(index - k, 0), 0, keepdims=False)
        total = total + passed_along(sent, "context", -k).astype(jnp.float32)
    return total


def carry_states(decay, state_term, reverse):
    direction = -1 if reverse else 1
    heads, width, states = state_term.shape
    state = state_term
    gain = decay
    entering = None
    entering_gain = None
    distance = 1
    contexts = lax.axis_size("context")
    while distance < contexts:
        high = gain.astype(jnp.bfloat16)
        rest = (gain - high.astype(jnp.float32)).astype(jnp.bfloat16)
        gains = jnp.zeros((16, states), jnp.bfloat16)
        gains = gains.at[0, :heads].set(high).at[1, :heads].set(rest)
        packed = jnp.concatenate(
            [state.astype(jnp.bfloat16).reshape(heads * width, states), gains], axis=0
        )
        got = passed_along(packed, "context", direction * distance)
        got_gain = (
            got[heads * width, :heads].astype(jnp.float32)
            + got[heads * width + 1, :heads].astype(jnp.float32)
        )
        got_state = got[: heads * width].astype(jnp.float32).reshape(heads, width, states)
        if entering is None:
            entering, entering_gain = got_state, got_gain
        else:
            entering = entering + entering_gain[:, None, None] * got_state
            entering_gain = entering_gain * got_gain
        state = state + gain[:, None, None] * got_state
        gain = gain * got_gain
        distance *= 2
    return entering


def per_device(
    tokens,
    lengths,
    deal,
    attn_norm_gain,
    ff_norm_gain,
    w_query,
    w_key,
    w_value,
    w_attn_out,
    w_gate_z,
    w_ssm_in,
    w_bc,
    w_step,
    w_ssm_out,
    conv_ssm,
    conv_bc,
    step_bias,
    decay_log,
    skip_gain,
    ssm_norm_gain,
    w_gate,
    w_up,
    w_down,
    cotangent,
):
    count_of_rows = tokens.shape[0]
    contexts = lax.axis_size("context")
    group_row_list = count_of_rows * contexts
    tensors = lax.axis_size("tensor")
    query_heads = QUERY_HEADS // tensors
    space_head_list = SPACE_HEADS // tensors
    inner_width_local = space_head_list * SPACE_HEAD_WIDTH
    score_scale = HEAD_WIDTH ** (-0.5)
    piece_rows = count_of_rows // contexts
    shift_amount = (deal[0, 0] // piece_rows - lax.axis_index("context")) % contexts
    shard = lax.axis_index("fsdp")
    own_inputs = jnp.concatenate(
        [w_query, w_key, w_value, w_gate_z, w_ssm_in, w_bc, w_step], axis=1
    )
    w_inputs = gather_shards(own_inputs)
    tokens_placed = relative(deal_rows(tokens, shift_amount), shard, 1)
    cot_placed = relative(deal_rows(cotangent, shift_amount), shard, 1)
    full_out = gather_shards(jnp.concatenate([w_attn_out, w_ssm_out], axis=1))
    full_gate_up = gather_shards(jnp.concatenate([w_gate, w_up], axis=1))
    full_down = gather_shards(w_down)
    attn_gain_rel = relative(attn_norm_gain, shard, 0)
    ff_gain_rel = relative(ff_norm_gain, shard, 0)
    query_end = query_heads * HEAD_WIDTH
    key_end = query_end + HEAD_WIDTH
    value_end = key_end + HEAD_WIDTH
    gate_end = value_end + inner_width_local
    ssm_end = gate_end + inner_width_local
    bc_end = ssm_end + 2 * STATE_WIDTH
    step_end = bc_end + space_head_list
    offset_rows = lax.axis_index("context") * count_of_rows
    positions = offset_rows + jnp.arange(count_of_rows, dtype=jnp.int32)
    lengths_row = lengths[0]
    segment_rows, starts = segments_of(lengths_row, positions)
    sequence_position = positions - starts
    ext_positions = offset_rows - (KC - 1) + jnp.arange(count_of_rows + KC - 1, dtype=jnp.int32)
    seg_extended, ext_starts = segments_of(lengths_row, ext_positions)
    segment_before = jnp.where(offset_rows > 0, seg_extended[KC - 2], -1)
    tokens_f = tokens_placed.astype(jnp.float32)
    inv_first = lax.rsqrt(jnp.mean(tokens_f * tokens_f, axis=-1, keepdims=True) + epsilon)
    scaled_first = tokens_f * inv_first
    normed = (scaled_first * attn_gain_rel).astype(jnp.bfloat16)
    projected = matmul_low(normed, w_inputs)
    query_pre = projected[:, :query_end]
    key_before_rotary = projected[:, query_end:key_end]
    value_low = projected[:, key_end:value_end].astype(jnp.bfloat16)
    gate_z = projected[:, value_end:gate_end]
    conv_in = projected[:, gate_end:bc_end].astype(jnp.bfloat16)
    step_raw = projected[:, bc_end:step_end]
    query_rot = apply_rotary(query_pre, sequence_position, query_heads, 1.0).astype(jnp.bfloat16)
    key_rot = apply_rotary(key_before_rotary, sequence_position, 1, 1.0).astype(jnp.bfloat16)
    key_value = gather_earlier(jnp.concatenate([key_rot, value_low], axis=1)).reshape(
        group_row_list, 2 * HEAD_WIDTH
    )
    query_matrix = (
        query_rot.reshape(count_of_rows, query_heads, HEAD_WIDTH)
        .transpose(1, 0, 2)
        .reshape(query_heads * count_of_rows, HEAD_WIDTH)
    )
    query_pos = jnp.tile(positions, query_heads)
    query_start = jnp.tile(starts, query_heads)
    query_rows = query_heads * count_of_rows
    block_row_list = min(512, group_row_list)
    block_count = group_row_list // block_row_list
    block_ids = jnp.arange(block_count, dtype=jnp.int32)

    def block_scores(block_index):
        block_first_row = block_index * block_row_list
        kv_piece = lax.dynamic_slice_in_dim(key_value, block_first_row, block_row_list, 0)
        key_pos = block_first_row + jnp.arange(block_row_list, dtype=jnp.int32)
        allowed = (key_pos[None, :] <= query_pos[:, None]) & (
            key_pos[None, :] >= query_start[:, None]
        )
        raw_scores = matmul_nt(query_matrix, kv_piece[:, :HEAD_WIDTH]) * score_scale
        return (kv_piece, allowed, raw_scores)

    def needed(block_index):
        block_first_row = block_index * block_row_list
        return (block_first_row <= positions[count_of_rows - 1]) & (
            block_first_row + block_row_list - 1 >= starts[0]
        )

    def max_step(carry, block_index):

        def max_compute(state_pair):
            running_max, running_sum = state_pair
            kv_piece, allowed, raw_scores = block_scores(block_index)
            masked = jnp.where(allowed, raw_scores, masked_value)
            new_max = jnp.maximum(running_max, jnp.max(masked, axis=1))
            exps = jnp.where(allowed, jnp.exp(masked - new_max[:, None]), 0.0)
            return (new_max, running_sum * jnp.exp(running_max - new_max) + jnp.sum(exps, axis=1))

        return (
            lax.cond(needed(block_index), max_compute, lambda state_pair: state_pair, carry),
            None,
        )

    start_pair = (
        jnp.full((query_rows,), masked_value, jnp.float32),
        jnp.zeros((query_rows,), jnp.float32),
    )
    (running_max, running_sum), unused_max = lax.scan(max_step, start_pair, block_ids)
    log_sum = running_max + jnp.log(running_sum)

    def out_step(summed, block_index):

        def out_compute(partial_sum):
            kv_piece, allowed, raw_scores = block_scores(block_index)
            prob_values = jnp.where(allowed, jnp.exp(raw_scores - log_sum[:, None]), 0.0)
            return partial_sum + matmul_low(
                prob_values.astype(jnp.bfloat16), kv_piece[:, HEAD_WIDTH:]
            )

        return (
            lax.cond(needed(block_index), out_compute, lambda partial_sum: partial_sum, summed),
            None,
        )

    attn_rows, unused_out = lax.scan(
        out_step, jnp.zeros((query_rows, HEAD_WIDTH), jnp.float32), block_ids
    )
    attended = (
        attn_rows.reshape(query_heads, count_of_rows, HEAD_WIDTH)
        .transpose(1, 0, 2)
        .reshape(count_of_rows, query_end)
        .astype(jnp.bfloat16)
    )
    halo_rows = passed_along(conv_in[count_of_rows - (KC - 1) :], "context", 1)
    extended = jnp.concatenate([halo_rows, conv_in], axis=0).astype(jnp.float32)
    conv_weight = jnp.concatenate([conv_ssm, conv_bc], axis=0)

    def mixer_piece(ext_values, conv_values, raw_steps, bias_values, decay_values, skip_values):
        return mixer_local(
            ext_values,
            conv_values,
            raw_steps,
            bias_values,
            decay_values,
            skip_values,
            seg_extended,
            segment_rows,
            segment_before,
            space_head_list,
        )

    (local_out, carry_gain, output_matrix, whole_decay, fresh_state), pullback = jax.vjp(
        mixer_piece, extended, conv_weight, step_raw, step_bias, decay_log, skip_gain
    )
    state_in = carry_states(whole_decay, fresh_state, False)
    carried = jnp.einsum("hpn,tn->thp", state_in, output_matrix, precision=highest)
    ssm_y = (local_out + carry_gain[:, :, None] * carried).reshape(count_of_rows, inner_width_local)
    silu_gate_values = jax.nn.silu(gate_z)
    gated = ssm_y * silu_gate_values
    square_sum = over_tensor(jnp.sum(gated * gated, axis=1))
    gated_inv = lax.rsqrt(square_sum / DI + epsilon)
    gated_norm = gated * gated_inv[:, None]
    mixed = (gated_norm * ssm_norm_gain).astype(jnp.bfloat16)
    both = jnp.concatenate([attended, mixed], axis=1)
    mixer = over_tensor(matmul_nt(both, full_out))
    resid = tokens_f + mixer
    inv_second = lax.rsqrt(jnp.mean(resid * resid, axis=-1, keepdims=True) + epsilon)
    scaled_second = resid * inv_second
    normed_ff = (scaled_second * ff_gain_rel).astype(jnp.bfloat16)
    gate_up = matmul_low(normed_ff, full_gate_up)
    hidden_width = gate_up.shape[1] // 2
    gate_v = gate_up[:, :hidden_width]
    up_v = gate_up[:, hidden_width:]
    sig_gate = jax.nn.sigmoid(gate_v)
    silu_gate = gate_v * sig_gate
    hidden = (silu_gate * up_v).astype(jnp.bfloat16)
    ff_part = over_tensor(matmul_nt(hidden, full_down))
    final = resid + ff_part
    output = relative(final.astype(jnp.bfloat16), shard, 1)
    grad_final = cot_placed.astype(jnp.float32)
    grad_ff = grad_final.astype(jnp.bfloat16)
    grad_hidden = matmul_low(grad_ff, full_down)
    grad_down = matmul_tn(grad_ff, hidden)
    grad_gate = (grad_hidden * up_v * sig_gate * (1.0 + gate_v * (1.0 - sig_gate))).astype(
        jnp.bfloat16
    )
    grad_up = (grad_hidden * silu_gate).astype(jnp.bfloat16)
    grad_gate_up = jnp.concatenate([grad_gate, grad_up], axis=1)
    grad_normed_ff = over_tensor(matmul_nt(grad_gate_up, full_gate_up))
    grad_weight_ff = jnp.concatenate([matmul_tn(normed_ff, grad_gate_up).astype(jnp.bfloat16), grad_down.astype(jnp.bfloat16)], axis=1)
    sum_ff = sum_context(scatter_sum(grad_weight_ff))
    grad_ff_gain = jnp.sum(grad_normed_ff * scaled_second, axis=0)
    grad_second = grad_normed_ff * ff_gain_rel
    grad_resid = (
        grad_final
        + inv_second * grad_second
        - resid * inv_second**3 * jnp.mean(grad_second * resid, axis=-1, keepdims=True)
    )
    grad_mixer = grad_resid.astype(jnp.bfloat16)
    grad_both = matmul_low(grad_mixer, full_out)
    grad_attended = grad_both[:, :query_end].astype(jnp.bfloat16)
    grad_mixed = grad_both[:, query_end:]
    grad_weight_out = matmul_tn(grad_mixer, both).astype(jnp.bfloat16)
    sum_out = sum_context(scatter_sum(grad_weight_out))
    grad_rows = (
        grad_attended.reshape(count_of_rows, query_heads, HEAD_WIDTH)
        .transpose(1, 0, 2)
        .reshape(query_rows, HEAD_WIDTH)
    )
    row_delta = jnp.sum(grad_rows.astype(jnp.float32) * attn_rows, axis=1)

    def back_step(grad_query, block_index):

        def back_compute(partial_grad):
            kv_piece, allowed, raw_scores = block_scores(block_index)
            prob_values = jnp.where(allowed, jnp.exp(raw_scores - log_sum[:, None]), 0.0)
            grad_probs = matmul_nt(grad_rows, kv_piece[:, HEAD_WIDTH:])
            grad_scores = (prob_values * (grad_probs - row_delta[:, None])).astype(jnp.bfloat16)
            partial_grad = (
                partial_grad + matmul_low(grad_scores, kv_piece[:, :HEAD_WIDTH]) * score_scale
            )
            grad_keys = matmul_tn(grad_scores, query_matrix) * score_scale
            grad_values = matmul_tn(prob_values.astype(jnp.bfloat16), grad_rows)
            return (partial_grad, jnp.concatenate([grad_keys, grad_values], axis=1))

        def skipped(partial_grad):
            return (partial_grad, jnp.zeros((block_row_list, 2 * HEAD_WIDTH), jnp.float32))

        return lax.cond(needed(block_index), back_compute, skipped, grad_query)

    grad_query_rows, grad_kv_blocks = lax.scan(
        back_step, jnp.zeros((query_rows, HEAD_WIDTH), jnp.float32), block_ids
    )
    grad_kv = scatter_earlier(grad_kv_blocks.reshape(contexts, count_of_rows, 2 * HEAD_WIDTH))
    grad_query_rot = (
        grad_query_rows.reshape(query_heads, count_of_rows, HEAD_WIDTH)
        .transpose(1, 0, 2)
        .reshape(count_of_rows, query_end)
    )
    grad_query_pre = apply_rotary(grad_query_rot, sequence_position, query_heads, -1.0).astype(
        jnp.bfloat16
    )
    grad_key_pre = apply_rotary(grad_kv[:, :HEAD_WIDTH], sequence_position, 1, -1.0).astype(
        jnp.bfloat16
    )
    grad_value = grad_kv[:, HEAD_WIDTH:].astype(jnp.bfloat16)
    sig_z = jax.nn.sigmoid(gate_z)
    grad_norm_in = grad_mixed * ssm_norm_gain
    grad_ssm_gain = jnp.sum(grad_mixed * gated_norm, axis=0)
    inner_sum = over_tensor(jnp.sum(grad_norm_in * gated, axis=1))
    gated_gradient = (
        gated_inv[:, None] * grad_norm_in - gated * (gated_inv**3 * inner_sum / DI)[:, None]
    )
    output_gradient = (gated_gradient * silu_gate_values).reshape(
        count_of_rows, space_head_list, SPACE_HEAD_WIDTH
    )
    grad_z = (gated_gradient * ssm_y * sig_z * (1.0 + gate_z * (1.0 - sig_z))).astype(jnp.bfloat16)
    grad_carry_gain = jnp.sum(output_gradient * carried, axis=2)
    weighted = carry_gain[:, :, None] * output_gradient
    grad_cmat_extra = jnp.einsum("thp,hpn->tn", weighted, state_in, precision=highest)
    back_term = jnp.einsum("thp,tn->hpn", weighted, output_matrix, precision=highest)
    grad_state_out = carry_states(whole_decay, back_term, True)
    grad_decay = jnp.sum(grad_state_out * state_in, axis=(1, 2))
    grad_ext, grad_conv, grad_step_raw, grad_bias, grad_decay_log, grad_skip = pullback(
        (output_gradient, grad_carry_gain, grad_cmat_extra, grad_decay, grad_state_out)
    )
    ext_rows = count_of_rows + KC - 1
    packed = jnp.concatenate(
        [grad_ext[:, inner_width_local:], grad_conv[inner_width_local:].T], axis=0
    )
    summed_bc = over_tensor(packed)
    grad_ext_full = jnp.concatenate([grad_ext[:, :inner_width_local], summed_bc[:ext_rows]], axis=1)
    grad_conv_bc = summed_bc[ext_rows:].T
    halo_grads = passed_along(grad_ext_full[: KC - 1], "context", -1)
    grad_conv_in = grad_ext_full[KC - 1 :] + jnp.concatenate(
        [jnp.zeros((count_of_rows - (KC - 1), grad_ext_full.shape[1]), jnp.float32), halo_grads],
        axis=0,
    )
    grad_inputs = jnp.concatenate(
        [
            grad_query_pre,
            grad_key_pre,
            grad_value,
            grad_z,
            grad_conv_in.astype(jnp.bfloat16),
            grad_step_raw.astype(jnp.bfloat16),
        ],
        axis=1,
    )
    column_scale = jnp.concatenate(
        [
            jnp.ones((ssm_end,), jnp.bfloat16),
            jnp.full((2 * STATE_WIDTH,), 0.5, jnp.bfloat16),
            jnp.ones((space_head_list,), jnp.bfloat16),
        ]
    )
    w_back = w_inputs * column_scale[None, :]
    grad_normed = over_tensor(matmul_nt(grad_inputs, w_back))
    grad_inputs_weight = matmul_tn(normed, grad_inputs).astype(jnp.bfloat16)
    sum_inputs = sum_context(scatter_sum(grad_inputs_weight))
    grad_attn_gain = jnp.sum(grad_normed * scaled_first, axis=0)
    grad_first = grad_normed * attn_gain_rel
    input_grad = relative(
        grad_resid
        + inv_first * grad_first
        - tokens_f * inv_first**3 * jnp.mean(grad_first * tokens_f, axis=-1, keepdims=True),
        shard,
        1,
    )
    stats_part = jnp.stack(
        [jnp.sum(final * final), jnp.sum(mixer * mixer), jnp.sum(ff_part * ff_part)]
    )
    small = [
        stats_part,
        relative(grad_attn_gain, shard, 0),
        relative(grad_ff_gain, shard, 0),
        grad_conv[:inner_width_local],
        grad_conv_bc,
        grad_bias,
        grad_decay_log,
        grad_skip,
        grad_ssm_gain,
    ]
    flat = jnp.concatenate([item.reshape(-1) for item in small])
    flat = jnp.pad(flat, (0, -flat.shape[0] % 1024)).reshape(-1, 128)
    flat = sum_small(flat).reshape(-1)
    summed = []
    at = 0
    for item in small:
        summed.append(flat[at : at + item.size].reshape(item.shape))
        at += item.size
    (
        stats_sum,
        sum_attn_gain,
        sum_ff_gain,
        sum_conv_ssm,
        sum_conv_bc,
        sum_bias,
        sum_decay_log,
        sum_skip,
        sum_ssm_gain,
    ) = summed
    token_count = group_row_list * lax.axis_size("fsdp")
    rms_stats = jnp.sqrt(stats_sum / (token_count * D))
    sum_inputs = sum_inputs.astype(jnp.float32)
    sum_out = sum_out.astype(jnp.float32)
    sum_ff = sum_ff.astype(jnp.float32)
    return (
        output,
        input_grad,
        sum_attn_gain,
        sum_ff_gain,
        sum_inputs[:, :query_end],
        sum_inputs[:, query_end:key_end],
        sum_inputs[:, key_end:value_end],
        sum_out[:, :query_end],
        sum_inputs[:, value_end:gate_end],
        sum_inputs[:, gate_end:ssm_end],
        sum_inputs[:, ssm_end:bc_end],
        sum_inputs[:, bc_end:step_end],
        sum_out[:, query_end:],
        sum_conv_ssm,
        sum_conv_bc,
        sum_bias,
        sum_decay_log,
        sum_skip,
        sum_ssm_gain,
        sum_ff[:, :hidden_width],
        sum_ff[:, hidden_width : 2 * hidden_width],
        sum_ff[:, 2 * hidden_width :],
        rms_stats,
    )


def solution(mesh):
    return jax.shard_map(
        per_device,
        mesh=mesh,
        in_specs=(
            P(("fsdp", "context"), None),
            P("fsdp", None),
            P("fsdp", "context"),
            P(),
            P(),
            P("fsdp", "tensor"),
            P("fsdp", "tensor"),
            P("fsdp", "tensor"),
            P("fsdp", "tensor"),
            P("fsdp", "tensor"),
            P("fsdp", "tensor"),
            P("fsdp", None),
            P("fsdp", "tensor"),
            P("fsdp", "tensor"),
            P("tensor", None),
            P(),
            P("tensor"),
            P("tensor"),
            P("tensor"),
            P("tensor"),
            P("fsdp", "tensor"),
            P("fsdp", "tensor"),
            P("fsdp", "tensor"),
            P(("fsdp", "context"), None),
        ),
        out_specs=(
            P(("fsdp", "context"), None),
            P(("fsdp", "context"), None),
            P(),
            P(),
            P("fsdp", "tensor"),
            P("fsdp", "tensor"),
            P("fsdp", "tensor"),
            P("fsdp", "tensor"),
            P("fsdp", "tensor"),
            P("fsdp", "tensor"),
            P("fsdp", None),
            P("fsdp", "tensor"),
            P("fsdp", "tensor"),
            P("tensor", None),
            P(),
            P("tensor"),
            P("tensor"),
            P("tensor"),
            P("tensor"),
            P("fsdp", "tensor"),
            P("fsdp", "tensor"),
            P("fsdp", "tensor"),
            P(),
        ),
        check_vma=False,
    )
```

```python
import functools

import jax
import jax.numpy as jnp
from jax import lax
from jax.experimental import pallas as pl
from jax.experimental.pallas import tpu as pltpu
from jax.sharding import PartitionSpec as P

D = 1024
QUERY_HEADS = 8
HEAD_WIDTH = 64
SPACE_HEADS = 24
SPACE_HEAD_WIDTH = 64
STATE_WIDTH = 128
KC = 4
DI = 1536
SHARDS = 4
BLOCK = D // SHARDS
LANES = 128

epsilon = 1e-06
rope_base = 100000000000.0
masked_value = -1e30
highest = lax.Precision.HIGHEST
bf16 = jnp.bfloat16
f32 = jnp.float32


def dot(left, right, precision=None):
    return lax.dot_general(
        left, right, (((1,), (0,)), ((), ())), precision=precision, preferred_element_type=f32
    )


def dot_tn(left, right, precision=None):
    return lax.dot_general(
        left, right, (((0,), (0,)), ((), ())), precision=precision, preferred_element_type=f32
    )


def dot_nt(left, right, precision=None):
    return lax.dot_general(
        left, right, (((1,), (1,)), ((), ())), precision=precision, preferred_element_type=f32
    )


def sigmoid(value):
    return 1.0 / (1.0 + jnp.exp(-value))


def iota(shape, axis):
    return lax.broadcasted_iota(jnp.int32, shape, axis)


def starts_of(lens_ref, places):
    start = jnp.zeros_like(places)
    end = jnp.int32(0)
    for i in range(lens_ref.shape[1]):
        end = end + lens_ref[0, i]
        start = jnp.where(places >= end, end, start)
    return start


def first_place(rows):
    return lax.axis_index("context") * rows


def head_lanes(width):
    shape = (LANES, width)
    return (iota(shape, 1) // SPACE_HEAD_WIDTH == iota(shape, 0)).astype(f32)


def spread(per_head, width):
    return dot(per_head, head_lanes(width), highest)


def head_sums(value):
    return dot_nt(value, head_lanes(value.shape[1]), highest)


def turn(value, cosine, sine, sign):
    lane = iota(value.shape, 1)
    partner = jnp.where(
        lane % HEAD_WIDTH < HEAD_WIDTH // 2,
        -sign * pltpu.roll(value, LANES - HEAD_WIDTH // 2, 1),
        sign * pltpu.roll(value, HEAD_WIDTH // 2, 1),
    )
    return value * cosine + partner * sine


def put_columns(out_ref, value, rows=None):
    out_ref[...] = value


def run(body, outs, args, smem=(), scratch=(), flops=10**9, name=None):
    moved = sum(a.size * a.dtype.itemsize for a in args)
    moved += sum(o.size * o.dtype.itemsize for o in outs)
    result = pl.pallas_call(
        body,
        out_shape=tuple(outs),
        in_specs=[
            pl.BlockSpec(memory_space=pltpu.SMEM if i in smem else pltpu.VMEM)
            for i in range(len(args))
        ],
        out_specs=tuple(pl.BlockSpec(memory_space=pltpu.VMEM) for _ in outs),
        scratch_shapes=list(scratch),
        cost_estimate=pl.CostEstimate(flops=flops, bytes_accessed=moved, transcendentals=0),
        name=name,
    )(*args)
    return result


def arr(rows, columns, kind):
    return jax.ShapeDtypeStruct((rows, columns), kind)


def passed_along(block, axis, distance):
    devices = range(lax.axis_size(axis))
    route = [(i - distance, i) for i in devices if i - distance in devices]
    return lax.ppermute(block, axis, route)


def swap(block, axis, bit):
    route = [(i, i ^ bit) for i in range(lax.axis_size(axis))]
    return lax.ppermute(block, axis, route)


def gather_shards(own):
    half = own.shape[0] // 2
    from_x = swap(own, "fsdp", 1)
    from_y = swap(own, "fsdp", 2)
    top = swap(from_x[:half], "fsdp", 2)
    low = swap(from_y[half:], "fsdp", 1)
    return (own, from_x, from_y, top, low)


def piece_columns(pieces):
    at = 0
    spans = []
    for piece in pieces:
        spans.append((at, at + piece.shape[0]))
        at += piece.shape[0]
    return spans


def grad_shapes(columns):
    half = BLOCK // 2
    return [arr(BLOCK, columns, bf16)] + [arr(half, columns, bf16)] * 6


def store_grad(refs, columns, left, right):
    refs[0][:, columns] = dot_tn(left[:, :BLOCK], right).astype(bf16)
    for k in range(1, SHARDS):
        value = dot_tn(left[:, k * BLOCK : (k + 1) * BLOCK], right).astype(bf16)
        refs[2 * k - 1][:, columns] = value[: BLOCK // 2]
        refs[2 * k][:, columns] = value[BLOCK // 2 :]


def plus_kernel(a_ref, b_ref, out_ref):
    out_ref[...] = (a_ref[...].astype(f32) + b_ref[...].astype(f32)).astype(bf16)


def plus(left, right):
    return run(plus_kernel, [arr(*left.shape, bf16)], (left, right), flops=left.size, name="plus")[0]


def split_store(total, bit, kept_ref, sent_ref):
    half = total.shape[0] // 2
    upper = (lax.axis_index("context") & bit) != 0

    @pl.when(upper)
    def _():
        kept_ref[...] = total[half:]
        sent_ref[...] = total[:half]

    @pl.when(jnp.logical_not(upper))
    def _():
        kept_ref[...] = total[:half]
        sent_ref[...] = total[half:]


def own_kernel(bit, own_ref, x0_ref, x1_ref, y0_ref, y1_ref, *out_refs):
    half = own_ref.shape[0] // 2
    parts = []
    for k, (x_ref, y_ref) in enumerate(((x0_ref, y0_ref), (x1_ref, y1_ref))):
        parts.append(
            own_ref[k * half : (k + 1) * half].astype(f32)
            + x_ref[...].astype(f32)
            + y_ref[...].astype(f32)
        )
    total = jnp.concatenate(parts, axis=0).astype(bf16)
    if bit:
        split_store(total, bit, *out_refs)
    else:
        out_refs[0][...] = total


def halve_kernel(bit, kept_ref, got_ref, *out_refs):
    total = (kept_ref[...].astype(f32) + got_ref[...].astype(f32)).astype(bf16)
    if bit:
        split_store(total, bit, *out_refs)
    else:
        out_refs[0][...] = total


def join_kernel(bit, own_ref, other_ref, out_ref):
    upper = (lax.axis_index("context") & bit) != 0
    own, other = own_ref[...], other_ref[...]
    out_ref[...] = jnp.concatenate(
        [jnp.where(upper, other, own), jnp.where(upper, own, other)], axis=0
    )


def last_kernel(bit, widths, own_ref, other_ref, *out_refs):
    half = own_ref.shape[0]
    upper = (lax.axis_index("context") & bit) != 0
    own, other = own_ref[...].astype(f32), other_ref[...].astype(f32)
    low, high = jnp.where(upper, other, own), jnp.where(upper, own, other)
    at = 0
    for out_ref, width in zip(out_refs, widths, strict=True):
        out_ref[:half] = low[:, at : at + width]
        out_ref[half:] = high[:, at : at + width]
        at += width


def reduce_grad(blocks, widths):
    own, x0, x1, y0, y1, d0, d1 = blocks
    columns = own.shape[1]
    top = swap(d0, "fsdp", 2)
    low = swap(d1, "fsdp", 1)
    got_x1 = swap(x1, "fsdp", 1)
    got_y0 = swap(y0, "fsdp", 2)
    got_x0 = swap(plus(x0, top), "fsdp", 1)
    got_y1 = swap(plus(y1, low), "fsdp", 2)
    bits = []
    bit = 1
    while bit < lax.axis_size("context"):
        bits.append(bit)
        bit *= 2
    rows = own.shape[0]

    def outs_at(rows):
        return [arr(rows // 2, columns, bf16)] * 2

    kept, sent = run(
        functools.partial(own_kernel, bits[0]),
        outs_at(rows),
        (own, got_x0, got_x1, got_y0, got_y1),
        flops=own.size,
        name="own_sum",
    )
    for i, bit in enumerate(bits):
        got = swap(sent, "context", bit)
        rows //= 2
        if i + 1 < len(bits):
            kept, sent = run(
                functools.partial(halve_kernel, bits[i + 1]),
                outs_at(rows),
                (kept, got),
                flops=own.size,
                name="halve",
            )
        else:
            (total,) = run(
                functools.partial(halve_kernel, 0),
                [arr(rows, columns, bf16)],
                (kept, got),
                flops=own.size,
                name="halve",
            )
    for bit in reversed(bits[1:]):
        other = swap(total, "context", bit)
        rows *= 2
        (total,) = run(
            functools.partial(join_kernel, bit),
            [arr(rows, columns, bf16)],
            (total, other),
            flops=own.size,
            name="join",
        )
    other = swap(total, "context", bits[0])
    return run(
        functools.partial(last_kernel, bits[0], widths),
        [arr(2 * rows, width, f32) for width in widths],
        (total, other),
        flops=own.size,
        name="last",
    )


def sum_small(block):
    for axis in ("fsdp", "context"):
        bit = 1
        while bit < lax.axis_size(axis):
            block = block + swap(block, axis, bit)
            bit *= 2
    return block


def deal_rows(block, shift):
    contexts = lax.axis_size("context")
    pieces = block.reshape(contexts, block.shape[0] // contexts, block.shape[1])
    if contexts > 4:
        dealt = lax.all_to_all(pieces, "context", split_axis=0, concat_axis=0, tiled=True)
        return [jnp.roll(dealt, shift, axis=0).reshape(block.shape)]
    index = lax.axis_index("context")
    got = []
    for k in range(contexts):
        piece = lax.dynamic_index_in_dim(pieces, index ^ k, 0, keepdims=False)
        got.append(swap(piece, "context", k) if k else piece)
    return got


def place_rows(piece_refs, deal_ref, out_ref):
    shard = lax.axis_index("fsdp")
    contexts = len(piece_refs)
    rows = piece_refs[0].shape[0]
    index = lax.axis_index("context")
    shift = deal_ref[0, 0] // rows - index + contexts
    for q in range(contexts):
        source = lax.rem(q - shift + 2 * contexts, contexts) ^ index
        for k in range(contexts):

            @pl.when((source == k) if contexts > 1 else True)
            def _():
                for b in range(SHARDS):
                    at = pl.multiple_of((shard ^ b) * BLOCK, BLOCK)
                    out_ref[q * rows : (q + 1) * rows, b * BLOCK : (b + 1) * BLOCK] = piece_refs[
                        k
                    ][:, pl.ds(at, BLOCK)]


def unplace(out_ref, value):
    shard = lax.axis_index("fsdp")
    for b in range(SHARDS):
        at = pl.multiple_of((shard ^ b) * BLOCK, BLOCK)
        out_ref[:, pl.ds(at, BLOCK)] = value[:, b * BLOCK : (b + 1) * BLOCK]


def relative_row(ref):
    shard = lax.axis_index("fsdp")
    return jnp.concatenate(
        [ref[:, pl.ds(pl.multiple_of((shard ^ b) * BLOCK, BLOCK), BLOCK)] for b in range(SHARDS)],
        axis=1,
    )


GAIN_ROWS = 16


def pack_state(out_ref, state, gain_row):
    rows = state.shape[0]
    diagonal = (iota((GAIN_ROWS, LANES), 0) == iota((GAIN_ROWS, LANES), 1)).astype(f32) * gain_row
    gains = dot(diagonal, jnp.ones((LANES, LANES), f32), highest)
    high = gains.astype(bf16)
    out_ref[:rows] = state.astype(bf16)
    out_ref[rows : rows + GAIN_ROWS] = high
    out_ref[rows + GAIN_ROWS :] = (gains - high.astype(f32)).astype(bf16)


def gains_of(ref):
    rows = ref.shape[0] - 2 * GAIN_ROWS
    return ref[rows : rows + GAIN_ROWS].astype(f32) + ref[rows + GAIN_ROWS :].astype(f32)


def chain_state(near_ref, far_ref):
    rows = near_ref.shape[0] - 2 * GAIN_ROWS
    gains = gains_of(near_ref)
    parts = []
    for h in range(rows // SPACE_HEAD_WIDTH):
        at = slice(h * SPACE_HEAD_WIDTH, (h + 1) * SPACE_HEAD_WIDTH)
        parts.append(near_ref[at].astype(f32) + gains[h : h + 1] * far_ref[at].astype(f32))
    return jnp.concatenate(parts, axis=0)


def chain_kernel(near_ref, far_ref, out_ref):
    rows = near_ref.shape[0] - 2 * GAIN_ROWS
    out_ref[:rows] = chain_state(near_ref, far_ref).astype(bf16)
    gains = gains_of(near_ref) * gains_of(far_ref)
    high = gains.astype(bf16)
    out_ref[rows : rows + GAIN_ROWS] = high
    out_ref[rows + GAIN_ROWS :] = (gains - high.astype(f32)).astype(bf16)


def chain(near, far):
    return run(
        chain_kernel, [arr(*near.shape, bf16)], (near, far), flops=near.size, name="chain"
    )[0]


def relay(packed, direction):
    contexts = lax.axis_size("context")
    near = passed_along(packed, "context", direction)
    distance = 2
    whole = chain(packed, near) if contexts > 2 else packed
    while distance * 2 < contexts:
        far = passed_along(whole, "context", direction * distance)
        near = chain(near, far)
        whole = chain(whole, far)
        distance *= 2
    far = passed_along(whole, "context", direction * distance)
    return near, far


def place_kernel(count, deal_ref, *refs):
    place_rows(refs[:count], deal_ref, refs[count])


def project_kernel(counts, deal_ref, gain_ref, cos_ref, sin_ref, *refs):
    piece_count, shard_count, edges = counts
    piece_refs = refs[:piece_count]
    shard_refs = refs[piece_count : piece_count + shard_count]
    x_ref, normed_ref, q_ref, kv_ref, z_ref, conv_ref, step_ref = refs[piece_count + shard_count :]
    query_end, kv_end, z_end, conv_end, step_end = edges
    place_rows(piece_refs, deal_ref, x_ref)
    x = x_ref[...].astype(f32)
    inverse = lax.rsqrt(jnp.mean(x * x, axis=1, keepdims=True) + epsilon)
    normed_ref[...] = (x * inverse * relative_row(gain_ref)).astype(bf16)

    def product(low, high):
        at = 0
        total = None
        for ref in shard_refs:
            rows = ref.shape[0]
            term = dot(normed_ref[:, at : at + rows], ref[:, low:high])
            total = term if total is None else total + term
            at += rows
        return total

    cosine, sine = cos_ref[...], sin_ref[...]
    query = product(0, query_end)
    for at in range(0, query_end, LANES):
        q_ref[:, at : at + LANES] = turn(query[:, at : at + LANES], cosine, sine, 1.0).astype(bf16)
    kv = product(query_end, kv_end)
    lane = iota(kv.shape, 1)
    kv_ref[...] = jnp.where(lane < HEAD_WIDTH, turn(kv, cosine, sine, 1.0), kv).astype(bf16)
    z_ref[...] = product(kv_end, z_end)
    conv_ref[...] = product(z_end, conv_end).astype(bf16)
    step_ref[...] = jnp.zeros(step_ref.shape, f32)
    step_ref[:, : step_end - conv_end] = product(conv_end, step_end)


def convolve(lens_ref, ext_ref, taps_ref, rows):
    base = first_place(rows)
    places = base + iota((rows, 1), 0)
    offset = places - starts_of(lens_ref, places)
    total = None
    for j in range(KC):
        window = ext_ref[8 - (KC - 1) + j : 8 - (KC - 1) + j + rows]
        if j < KC - 1:
            window = jnp.where(offset >= KC - 1 - j, window, 0.0)
        term = window * taps_ref[j : j + 1]
        total = term if total is None else total + term
    return total


def decays(lens_ref, step_raw, params_ref, rows):
    base = first_place(rows)
    raw = step_raw + params_ref[0:1]
    step = jnp.maximum(raw, 0.0) + jnp.log(1.0 + jnp.exp(-jnp.abs(raw)))
    rate = -jnp.exp(params_ref[1:2])
    lower = (iota((rows, rows), 0) >= iota((rows, rows), 1)).astype(f32)
    cumulative = dot(lower, step * rate, highest)
    places = base + iota((rows, 1), 0)
    start = starts_of(lens_ref, places)
    carry = jnp.where(start < base, jnp.exp(cumulative), 0.0)
    last_start = starts_of(lens_ref, base + rows - 1)
    last = cumulative[rows - 1 : rows]
    tail = jnp.where(places >= last_start, jnp.exp(last - cumulative), 0.0)
    return raw, step, rate, cumulative, carry, tail


def joined_mask(lens_ref, rows):
    base = first_place(rows)
    start = starts_of(lens_ref, base + iota((rows, 1), 0)) - base
    key = iota((rows, rows), 1)
    return (key <= iota((rows, rows), 0)) & (key >= start)


def head_decay(h, cum_ref, cum_t_ref, masked):
    lane = iota(cum_ref.shape, 1)
    column = jnp.sum(jnp.where(lane == h, cum_ref[...], 0.0), axis=1, keepdims=True)
    return jnp.exp(column - cum_t_ref[pl.ds(h, 1), :] + masked)


def space_kernel(
    lens_ref,
    conv_ref,
    halo_ref,
    step_ref,
    taps_ref,
    params_ref,
    act_ref,
    y_ref,
    packed_ref,
    cum_ref,
    ext_ref,
    scaled_ref,
    cum_t_ref,
    inner_ref,
    mask_ref,
):
    rows, width = conv_ref.shape
    inner = width - 2 * STATE_WIDTH
    ext_ref[0:8] = halo_ref[...].astype(f32)
    ext_ref[8:] = conv_ref[...].astype(f32)
    before = convolve(lens_ref, ext_ref, taps_ref, rows)
    act_ref[...] = before * sigmoid(before)
    raw, step, rate, cumulative, carry, tail = decays(lens_ref, step_ref[...], params_ref, rows)
    cum_ref[...] = cumulative
    cum_t_ref[...] = jnp.transpose(cumulative)
    u = act_ref[:, :inner]
    scaled = u * spread(step, inner)
    scaled_ref[...] = scaled.astype(bf16)
    bmat = act_ref[:, inner : inner + STATE_WIDTH].astype(bf16)
    cmat = act_ref[:, inner + STATE_WIDTH :].astype(bf16)
    tailed = (scaled * spread(tail, inner)).astype(bf16)
    pack_state(packed_ref, dot_tn(tailed, bmat), carry[rows - 1 : rows])
    inner_ref[...] = dot_nt(cmat, bmat)
    mask_ref[...] = jnp.where(joined_mask(lens_ref, rows), 0.0, masked_value)
    y_ref[...] = spread(params_ref[...], inner)[2:3] * u

    def pair(p, carried):
        at = pl.multiple_of(p * LANES, LANES)
        block = scaled_ref[:, pl.ds(at, LANES)]
        outs = []
        for i in range(2):
            decay = head_decay(2 * p + i, cum_ref, cum_t_ref, mask_ref[...])
            outs.append(dot((decay * inner_ref[...]).astype(bf16), block))
        lane = iota((rows, LANES), 1)
        y_ref[:, pl.ds(at, LANES)] += jnp.where(lane < SPACE_HEAD_WIDTH, outs[0], outs[1])
        return carried

    lax.fori_loop(0, inner // LANES, pair, 0)


def gate_kernel(
    lens_ref, near_ref, far_ref, act_ref, y_ref, cum_ref, z_ref, state_ref, carried_ref, ssm_ref, square_ref
):
    rows, inner = y_ref.shape
    state = chain_state(near_ref, far_ref).astype(bf16)
    state_ref[...] = state
    cmat = act_ref[:, inner + STATE_WIDTH :].astype(bf16)
    carried = dot_nt(cmat, state)
    carried_ref[...] = carried
    base = first_place(rows)
    start = starts_of(lens_ref, base + iota((rows, 1), 0))
    carry = jnp.where(start < base, jnp.exp(cum_ref[...]), 0.0)
    ssm_y = y_ref[...] + spread(carry, inner) * carried
    ssm_ref[...] = ssm_y
    z = z_ref[...]
    gated = ssm_y * z * sigmoid(z)
    square_ref[...] = jnp.broadcast_to(jnp.sum(gated * gated, axis=1, keepdims=True), (rows, LANES))


def mix_kernel(
    attended_ref, ssm_ref, z_ref, square_ref, other_ref, gain_ref, *refs
):
    shard_refs, (both_ref, part_ref) = refs[:-2], refs[-2:]
    width = attended_ref.shape[1]
    z = z_ref[...]
    gated = ssm_ref[...] * z * sigmoid(z)
    inverse = lax.rsqrt((square_ref[:, :1] + other_ref[:, :1]) / DI + epsilon)
    both_ref[:, :width] = attended_ref[...]
    both_ref[:, width:] = (gated * inverse * gain_ref[...]).astype(bf16)
    at = 0
    for ref in shard_refs:
        part_ref[:, at : at + ref.shape[0]] = dot_nt(both_ref[...], ref[...])
        at += ref.shape[0]


def hidden_kernel(x_ref, part_ref, other_ref, gain_ref, *refs):
    shard_refs = refs[:-4]
    mixer_ref, normed_ref, gate_ref, up_ref = refs[-4:]
    mixer = part_ref[...] + other_ref[...]
    mixer_ref[...] = mixer
    resid = x_ref[...].astype(f32) + mixer
    inverse = lax.rsqrt(jnp.mean(resid * resid, axis=1, keepdims=True) + epsilon)
    normed_ref[...] = (resid * inverse * relative_row(gain_ref)).astype(bf16)
    width = gate_ref.shape[1]
    for out_ref, low in ((gate_ref, 0), (up_ref, width)):
        at = 0
        total = None
        for ref in shard_refs:
            rows = ref.shape[0]
            term = dot(normed_ref[:, at : at + rows], ref[:, low : low + width])
            total = term if total is None else total + term
            at += rows
        out_ref[...] = total


def down_kernel(counts, gate_ref, up_ref, cot_ref, *refs):
    count = counts
    gate_up_refs, down_refs = refs[:count], refs[count : 2 * count]
    hidden_ref, pair_ref, part_ref, back_ref = refs[2 * count :]
    width = gate_ref.shape[1]
    gate = gate_ref[...]
    up = up_ref[...]
    sig = sigmoid(gate)
    silu = gate * sig
    hidden_ref[...] = (silu * up).astype(bf16)
    at = 0
    grad_hidden = None
    for ref in down_refs:
        rows = ref.shape[0]
        term = dot(cot_ref[:, at : at + rows], ref[...])
        grad_hidden = term if grad_hidden is None else grad_hidden + term
        at += rows
    pair_ref[:, :width] = (grad_hidden * up * sig * (1.0 + gate * (1.0 - sig))).astype(bf16)
    pair_ref[:, width:] = (grad_hidden * silu).astype(bf16)
    at = 0
    for ref, down in zip(gate_up_refs, down_refs, strict=True):
        rows = ref.shape[0]
        back_ref[:, at : at + rows] = dot_nt(pair_ref[...], ref[...])
        part_ref[:, at : at + rows] = dot_nt(hidden_ref[...], down[...])
        at += rows


def final_kernel(x_ref, mixer_ref, part_ref, other_ref, out_ref, stats_ref):
    mixer = mixer_ref[...]
    ff_part = part_ref[...] + other_ref[...]
    final = x_ref[...].astype(f32) + mixer + ff_part
    unplace(out_ref, final.astype(bf16))
    lane = iota((8, LANES), 1)
    stats = jnp.zeros((8, LANES), f32)
    for i, value in enumerate((final, mixer, ff_part)):
        total = jnp.sum(jnp.sum(value * value, axis=0, keepdims=True), axis=1, keepdims=True)
        stats = jnp.where(lane == i, total, stats)
    stats_ref[...] = stats


def head_pair(ref, h, rows):
    at = h // 2 * LANES
    lane = iota((rows, LANES), 1)
    mine = (lane < HEAD_WIDTH) if h % 2 == 0 else (lane >= HEAD_WIDTH)
    value = ref[:, at : at + LANES]
    return jnp.where(mine, value, jnp.zeros_like(value))


def doubled(kv):
    lane = iota(kv.shape, 1)
    wide = kv.astype(f32)
    turned = pltpu.roll(wide, HEAD_WIDTH, 1)
    keys = jnp.where(lane < HEAD_WIDTH, wide, turned).astype(bf16)
    values = jnp.where(lane < HEAD_WIDTH, turned, wide).astype(bf16)
    return keys, values


def allowed_mask(lens_ref, rows, key_base):
    places = first_place(rows) + iota((rows, 1), 0)
    start = starts_of(lens_ref, places)
    key = key_base + iota((rows, rows), 1)
    return (key <= places) & (key >= start)


def over_blocks(lens_ref, rows, kv_refs, body, skipped):
    base = first_place(rows)
    first_start = starts_of(lens_ref, base)
    if len(kv_refs) == 1 and len(kv_refs[0].shape) == 3:

        def step(k, carried):
            key_base = k * rows
            seen = (key_base <= base) & (key_base + rows > first_start)

            @pl.when(seen)
            def _():
                body(k, kv_refs[0][k], key_base)

            @pl.when(jnp.logical_not(seen))
            def _():
                skipped(k)

            return carried

        lax.fori_loop(0, kv_refs[0].shape[0], step, 0)
        return
    for k, ref in enumerate(kv_refs):
        key_base = base - k * rows
        seen = (key_base >= 0) & (key_base + rows > first_start)

        @pl.when(seen)
        def _():
            body(k, ref[...], key_base)

        @pl.when(jnp.logical_not(seen))
        def _():
            skipped(k)


def attend_kernel(count, lens_ref, q_ref, *refs):
    kv_refs = refs[:count]
    out_ref, exact_ref, log_ref, max_ref, sum_ref, acc_ref = refs[count:]
    rows, width = q_ref.shape
    heads = width // HEAD_WIDTH
    max_ref[...] = jnp.full(max_ref.shape, masked_value, f32)
    sum_ref[...] = jnp.zeros(sum_ref.shape, f32)
    acc_ref[...] = jnp.zeros(acc_ref.shape, f32)

    def body(k, kv, key_base):
        keys, values = doubled(kv)
        allowed = allowed_mask(lens_ref, rows, key_base)
        for h in range(heads):
            scores = dot_nt(head_pair(q_ref, h, rows), keys) * HEAD_WIDTH**-0.5
            scores = jnp.where(allowed, scores, masked_value)
            old = max_ref[h]
            new = jnp.maximum(old, jnp.max(scores, axis=1, keepdims=True))
            weights = jnp.where(allowed, jnp.exp(scores - new[:, :1]), 0.0)
            scale = jnp.exp(old - new)
            max_ref[h] = new
            sum_ref[h] = sum_ref[h] * scale + jnp.sum(weights, axis=1, keepdims=True)
            acc_ref[h] = acc_ref[h] * scale + dot(weights.astype(bf16), values)

    over_blocks(lens_ref, rows, kv_refs, body, lambda k: None)
    lane = iota((rows, LANES), 1)
    for pair in range(heads // 2):
        halves = []
        for h in (2 * pair, 2 * pair + 1):
            log_ref[h] = max_ref[h] + jnp.log(sum_ref[h])
            halves.append(acc_ref[h] / sum_ref[h])
        value = jnp.where(lane < HEAD_WIDTH, halves[0], halves[1])
        exact_ref[:, pair * LANES : (pair + 1) * LANES] = value
        out_ref[:, pair * LANES : (pair + 1) * LANES] = value.astype(bf16)


def attend_back_kernel(count, lens_ref, q_ref, grad_ref, exact_ref, log_ref, cos_ref, sin_ref, *refs):
    kv_refs = refs[:count]
    query_ref = refs[count]
    kv_grad_refs = refs[count + 1 : -2]
    delta_ref, acc_ref = refs[-2:]
    rows, width = q_ref.shape
    heads = width // HEAD_WIDTH
    scale = HEAD_WIDTH**-0.5
    acc_ref[...] = jnp.zeros(acc_ref.shape, f32)
    lane = iota((rows, LANES), 1)
    for h in range(heads):
        at = h // 2 * LANES
        product = head_pair(grad_ref, h, rows).astype(f32) * exact_ref[:, at : at + LANES]
        delta_ref[h] = jnp.broadcast_to(jnp.sum(product, axis=1, keepdims=True), (rows, LANES))

    def store(k, value):
        if len(kv_grad_refs) == 1 and len(kv_grad_refs[0].shape) == 3:
            kv_grad_refs[0][k] = value.astype(kv_grad_refs[0].dtype)
        else:
            kv_grad_refs[k][...] = value.astype(kv_grad_refs[k].dtype)

    def body(k, kv, key_base):
        keys, values = doubled(kv)
        allowed = allowed_mask(lens_ref, rows, key_base)
        grad_keys = jnp.zeros((rows, LANES), f32)
        grad_values = jnp.zeros((rows, LANES), f32)
        for h in range(heads):
            query = head_pair(q_ref, h, rows)
            grad = head_pair(grad_ref, h, rows)
            scores = dot_nt(query, keys) * scale
            probs = jnp.where(allowed, jnp.exp(scores - log_ref[h][:, :1]), 0.0)
            grad_probs = dot_nt(grad, values)
            grad_scores = (probs * (grad_probs - delta_ref[h][:, :1])).astype(bf16)
            acc_ref[h] += dot(grad_scores, keys)
            grad_keys += dot_tn(grad_scores, query)
            grad_values += dot_tn(probs.astype(bf16), grad)
        grad_keys = (grad_keys + pltpu.roll(grad_keys, HEAD_WIDTH, 1)) * scale
        grad_values = grad_values + pltpu.roll(grad_values, HEAD_WIDTH, 1)
        store(k, jnp.where(lane < HEAD_WIDTH, grad_keys, grad_values))

    over_blocks(
        lens_ref, rows, kv_refs, body, lambda k: store(k, jnp.zeros((rows, LANES), f32))
    )
    for pair in range(heads // 2):
        value = jnp.where(lane < HEAD_WIDTH, acc_ref[2 * pair], acc_ref[2 * pair + 1]) * scale
        query_ref[:, pair * LANES : (pair + 1) * LANES] = turn(
            value, cos_ref[...], sin_ref[...], -1.0
        ).astype(bf16)


def norm_back(grad, value, inverse):
    return inverse * grad - value * (inverse * inverse * inverse) * jnp.mean(
        grad * value, axis=1, keepdims=True
    )


def resid_back_kernel(
    back_ref, other_ref, x_ref, mixer_ref, cot_ref, gain_ref, ssm_ref, z_ref, square_ref,
    square_other_ref, ssm_gain_ref, *refs
):
    shard_refs = refs[:-6]
    resid_ref, low_ref, attended_ref, mixed_ref, inner_ref, gains_ref = refs[-6:]
    rows = x_ref.shape[0]
    grad_normed = back_ref[...] + other_ref[...]
    resid = x_ref[...].astype(f32) + mixer_ref[...]
    inverse = lax.rsqrt(jnp.mean(resid * resid, axis=1, keepdims=True) + epsilon)
    ff_gain = jnp.sum(grad_normed * (resid * inverse), axis=0, keepdims=True)
    grad_resid = cot_ref[...].astype(f32) + norm_back(
        grad_normed * relative_row(gain_ref), resid, inverse
    )
    resid_ref[...] = grad_resid
    low_ref[...] = grad_resid.astype(bf16)
    width = attended_ref.shape[1]
    at = 0
    total = None
    for ref in shard_refs:
        count = ref.shape[0]
        term = dot(low_ref[:, at : at + count], ref[...])
        total = term if total is None else total + term
        at += count
    attended_ref[...] = total[:, :width].astype(bf16)
    grad_mixed = total[:, width:]
    mixed_ref[...] = grad_mixed
    z = z_ref[...]
    gated = ssm_ref[...] * z * sigmoid(z)
    gated_inverse = lax.rsqrt((square_ref[:, :1] + square_other_ref[:, :1]) / DI + epsilon)
    inner = jnp.sum(grad_mixed * ssm_gain_ref[...] * gated, axis=1, keepdims=True)
    inner_ref[...] = jnp.broadcast_to(inner, (rows, LANES))
    gains_ref[0:1] = ff_gain
    gains_ref[1:2, : grad_mixed.shape[1]] = jnp.sum(
        grad_mixed * (gated * gated_inverse), axis=0, keepdims=True
    )


def gate_back_kernel(
    lens_ref, mixed_ref, inner_ref, inner_other_ref, square_ref, square_other_ref, ssm_gain_ref,
    ssm_ref, z_ref, carried_ref, act_ref, cum_ref, state_ref,
    out_ref, z_grad_ref, packed_ref, cmat_ref, carry_ref,
):
    rows, inner = ssm_ref.shape
    z = z_ref[...]
    sig = sigmoid(z)
    ssm_y = ssm_ref[...]
    gated = ssm_y * z * sig
    inverse = lax.rsqrt((square_ref[:, :1] + square_other_ref[:, :1]) / DI + epsilon)
    total = (inner_ref[:, :1] + inner_other_ref[:, :1]) / DI
    grad_gated = inverse * (mixed_ref[...] * ssm_gain_ref[...]) - gated * (
        inverse * inverse * inverse * total
    )
    grad_out = grad_gated * (z * sig)
    out_ref[...] = grad_out
    z_grad_ref[...] = (grad_gated * ssm_y * sig * (1.0 + z * (1.0 - sig))).astype(bf16)
    base = first_place(rows)
    start = starts_of(lens_ref, base + iota((rows, 1), 0))
    carry = jnp.where(start < base, jnp.exp(cum_ref[...]), 0.0)
    weighted = (spread(carry, inner) * grad_out).astype(bf16)
    cmat = act_ref[:, inner + STATE_WIDTH :].astype(bf16)
    pack_state(packed_ref, dot_tn(weighted, cmat), carry[rows - 1 : rows])
    cmat_ref[...] = dot(weighted, state_ref[...])
    carry_ref[...] = head_sums(grad_out * carried_ref[...])


def space_back_kernel(
    lens_ref, grad_ref, act_ref, cum_ref, step_ref, params_ref, scaled_grad_ref, grad_inner_ref,
    scaled_ref, cum_t_ref, inner_ref, mask_ref, low_ref,
):
    rows, inner = grad_ref.shape
    raw = step_ref[...] + params_ref[0:1]
    step = jnp.maximum(raw, 0.0) + jnp.log(1.0 + jnp.exp(-jnp.abs(raw)))
    cum_t_ref[...] = jnp.transpose(cum_ref[...])
    scaled_ref[...] = (act_ref[:, :inner] * spread(step, inner)).astype(bf16)
    bmat = act_ref[:, inner : inner + STATE_WIDTH].astype(bf16)
    cmat = act_ref[:, inner + STATE_WIDTH :].astype(bf16)
    inner_ref[...] = dot_nt(cmat, bmat)
    mask_ref[...] = jnp.where(joined_mask(lens_ref, rows), 0.0, masked_value)
    low_ref[...] = grad_ref[...].astype(bf16)
    grad_inner_ref[...] = jnp.zeros(grad_inner_ref.shape, f32)

    def pair(p, carried):
        at = pl.multiple_of(p * LANES, LANES)
        block = scaled_ref[:, pl.ds(at, LANES)]
        grad = low_ref[:, pl.ds(at, LANES)]
        lane = iota((rows, LANES), 1)
        outs = []
        for i in range(2):
            decay = head_decay(2 * p + i, cum_ref, cum_t_ref, mask_ref[...])
            outs.append(dot_tn((decay * inner_ref[...]).astype(bf16), grad))
            mine = (lane < SPACE_HEAD_WIDTH) if i == 0 else (lane >= SPACE_HEAD_WIDTH)
            grad_inner_ref[...] += decay * dot_nt(
                jnp.where(mine, grad, jnp.zeros_like(grad)), block
            )
        scaled_grad_ref[:, pl.ds(at, LANES)] = jnp.where(
            lane < SPACE_HEAD_WIDTH, outs[0], outs[1]
        )
        return carried

    lax.fori_loop(0, inner // LANES, pair, 0)


def conv_back_kernel(
    lens_ref, near_ref, far_ref, grad_ref, scaled_grad_ref, grad_inner_ref, act_ref, y_ref, step_ref,
    conv_ref, halo_ref, taps_ref, params_ref, state_ref, cmat_grad_ref, carry_grad_ref,
    ssm_out_ref, bc_ref, halo_out_ref, halo_bc_ref, step_out_ref, tap_ref, small_ref,
    ext_ref, act_grad_ref,
):
    rows, inner = grad_ref.shape
    width = conv_ref.shape[1]
    base = first_place(rows)
    raw, step, rate, cumulative, carry, tail = decays(lens_ref, step_ref[...], params_ref, rows)
    state_grad = chain_state(near_ref, far_ref)
    low_state = state_grad.astype(bf16)
    bmat = act_ref[:, inner : inner + STATE_WIDTH].astype(bf16)
    cmat = act_ref[:, inner + STATE_WIDTH :].astype(bf16)
    u = act_ref[:, :inner]
    step_wide = spread(step, inner)
    tail_wide = spread(tail, inner)
    skip_wide = spread(params_ref[...], inner)[2:3]
    scaled = u * step_wide
    out_grad = grad_ref[...]
    from_state = dot_nt(bmat, low_state)
    scaled_local = scaled_grad_ref[...]
    scaled_grad = scaled_local + tail_wide * from_state
    tail_grad = head_sums(scaled * from_state) * tail
    grad_inner = grad_inner_ref[...].astype(bf16)
    act_grad_ref[8 : 8 + rows, :inner] = skip_wide * out_grad + scaled_grad * step_wide
    act_grad_ref[8 : 8 + rows, inner : inner + STATE_WIDTH] = dot_tn(grad_inner, cmat) + dot(
        (tail_wide * scaled).astype(bf16), low_state
    )
    act_grad_ref[8 : 8 + rows, inner + STATE_WIDTH :] = dot(grad_inner, bmat) + cmat_grad_ref[...]
    step_grad = head_sums(scaled_grad * u)
    local = y_ref[...] - skip_wide * u
    cum_grad = head_sums(
        out_grad.astype(bf16).astype(f32) * local - scaled.astype(bf16).astype(f32) * scaled_local
    )
    cum_grad = cum_grad + carry_grad_ref[...] * carry - tail_grad
    product = state_grad * state_ref[...].astype(f32)
    summed = dot_nt(jnp.ones((8, LANES), f32), product, highest)
    decay_grad = head_sums(summed)[0:1]
    ending = jnp.sum(tail_grad, axis=0, keepdims=True) + decay_grad * carry[rows - 1 : rows]
    upper = (iota((rows, rows), 0) <= iota((rows, rows), 1)).astype(f32)
    log_grad = dot(upper, cum_grad, highest) + ending
    step_grad = step_grad + log_grad * rate
    raw_grad = step_grad * sigmoid(raw)
    step_out_ref[...] = raw_grad.astype(bf16)
    small_ref[...] = jnp.zeros(small_ref.shape, f32)
    small_ref[0:1] = jnp.sum(raw_grad, axis=0, keepdims=True)
    small_ref[1:2] = jnp.sum(log_grad * step, axis=0, keepdims=True) * rate
    small_ref[2:3] = head_sums(jnp.broadcast_to(
        jnp.sum(out_grad * u, axis=0, keepdims=True), (8, inner)))[0:1]
    ext_ref[0:8] = halo_ref[...].astype(f32)
    ext_ref[8:] = conv_ref[...].astype(f32)
    before = convolve(lens_ref, ext_ref, taps_ref, rows)
    sig = sigmoid(before)
    inside = slice(8, 8 + rows)
    act_grad_ref[inside] = act_grad_ref[inside] * (sig * (1.0 + before * (1.0 - sig)))
    act_grad_ref[0:8] = jnp.zeros((8, width), f32)
    act_grad_ref[8 + rows :] = jnp.zeros((8, width), f32)
    tap_ref[...] = jnp.zeros(tap_ref.shape, f32)
    total = None
    for j in range(KC):
        back = KC - 1 - j
        places = base + iota((rows + 8, 1), 0) - 8 + back
        seen = places - starts_of(lens_ref, places) >= back
        window = jnp.where(seen, act_grad_ref[back : back + rows + 8], 0.0)
        term = window * taps_ref[j : j + 1]
        total = term if total is None else total + term
        tap_ref[j : j + 1] = jnp.sum(
            jnp.where(
                (base + iota((rows, 1), 0)) - starts_of(lens_ref, base + iota((rows, 1), 0)) >= back,
                act_grad_ref[inside],
                0.0,
            )
            * ext_ref[8 - back : 8 - back + rows],
            axis=0,
            keepdims=True,
        )
    ssm_out_ref[...] = total[8:, :inner]
    bc_ref[:rows] = total[8:, inner:]
    bc_ref[rows:] = tap_ref[:, inner:]
    halo_out_ref[...] = total[:8]
    halo_bc_ref[...] = total[:8, inner:]


def inputs_back_kernel(
    counts, ssm_ref, bc_ref, bc_other_ref, halo_ref, halo_bc_ref, step_ref, query_ref, z_ref,
    cos_ref, sin_ref, tap_ref, *refs
):
    kv_count, shard_count, edges = counts
    kv_refs = refs[:kv_count]
    shard_refs = refs[kv_count : kv_count + shard_count]
    early_ref, late_ref, back_ref, taps_ref = refs[kv_count + shard_count :]
    query_end, kv_end, z_end, conv_end, step_end = edges
    rows, inner = ssm_ref.shape
    kv = kv_refs[0][...].astype(f32)
    for ref in kv_refs[1:]:
        kv = kv + ref[...].astype(f32)
    lane = iota(kv.shape, 1)
    early_ref[:, :query_end] = query_ref[...]
    early_ref[:, query_end:kv_end] = jnp.where(
        lane < HEAD_WIDTH, turn(kv, cos_ref[...], sin_ref[...], -1.0), kv
    ).astype(bf16)
    early_ref[:, kv_end:] = z_ref[...]
    pad = jnp.zeros((rows - 8, inner), f32)
    late_ref[:, :inner] = (
        ssm_ref[...] + jnp.concatenate([pad, halo_ref[:, :inner]], axis=0)
    ).astype(bf16)
    bc = bc_ref[:rows] + bc_other_ref[:rows]
    pad = jnp.zeros((rows - 8, 2 * STATE_WIDTH), f32)
    bc_low = (
        bc + jnp.concatenate([pad, halo_ref[:, inner:] + halo_bc_ref[...]], axis=0)
    ).astype(bf16)
    late_ref[:, inner : inner + 2 * STATE_WIDTH] = bc_low
    late_ref[:, inner + 2 * STATE_WIDTH :] = step_ref[:, : step_end - conv_end]
    taps_ref[:, :inner] = tap_ref[:, :inner]
    taps_ref[:, inner:] = bc_ref[rows:] + bc_other_ref[rows:]
    half_bc = (bc_low.astype(f32) * 0.5).astype(bf16)
    at = 0
    for ref in shard_refs:
        count = ref.shape[0]
        total = dot_nt(early_ref[...], ref[:, :z_end])
        total = total + dot_nt(late_ref[:, :inner], ref[:, z_end : z_end + inner])
        total = total + dot_nt(half_bc, ref[:, z_end + inner : conv_end])
        total = total + dot_nt(late_ref[:, inner + 2 * STATE_WIDTH :], ref[:, conv_end:step_end])
        back_ref[:, at : at + count] = total
        at += count


def first_back_kernel(
    x_ref, resid_ref, back_ref, other_ref, gain_ref, gains_ref, taps_ref, small_ref, stats_ref,
    out_ref, sums_ref,
):
    x = x_ref[...].astype(f32)
    inverse = lax.rsqrt(jnp.mean(x * x, axis=1, keepdims=True) + epsilon)
    grad_normed = back_ref[...] + other_ref[...]
    unplace(
        out_ref,
        resid_ref[...] + norm_back(grad_normed * relative_row(gain_ref), x, inverse),
    )
    attn_gain = jnp.sum(grad_normed * (x * inverse), axis=0, keepdims=True)
    sums_ref[...] = jnp.zeros(sums_ref.shape, f32)
    unplace(sums_ref.at[0:1], attn_gain)
    unplace(sums_ref.at[1:2], gains_ref[0:1])
    inner = sums_ref.shape[1] - 2 * STATE_WIDTH
    sums_ref[2 : 2 + KC] = taps_ref[0:KC]
    sums_ref[6:7, :inner] = gains_ref[1:2, :inner]
    sums_ref[6:7, inner : inner + LANES] = small_ref[0:1]
    sums_ref[6:7, inner + LANES :] = small_ref[1:2]
    sums_ref[7:8, :LANES] = small_ref[2:3]
    sums_ref[7:8, LANES : 2 * LANES] = stats_ref[0:1]


def ff_grad_kernel(normed_ref, pair_ref, cot_ref, hidden_ref, *out_refs):
    width = pair_ref.shape[1]
    store_grad(out_refs, slice(0, width), normed_ref[...], pair_ref[...])
    store_grad(
        out_refs, slice(width, width + hidden_ref.shape[1]), cot_ref[...], hidden_ref[...]
    )


def weight_grad_kernel(left_ref, right_ref, *out_refs):
    store_grad(out_refs, slice(0, right_ref.shape[1]), left_ref[...], right_ref[...])


def per_device(
    tokens, lengths, deal, attn_norm_gain, ff_norm_gain, w_query, w_key, w_value, w_attn_out,
    w_gate_z, w_ssm_in, w_bc, w_step, w_ssm_out, conv_ssm, conv_bc, step_bias, decay_log,
    skip_gain, ssm_norm_gain, w_gate, w_up, w_down, cotangent,
):
    rows = tokens.shape[0]
    contexts = lax.axis_size("context")
    tensors = lax.axis_size("tensor")
    query_width = w_query.shape[1]
    inner = w_ssm_in.shape[1]
    heads = inner // SPACE_HEAD_WIDTH
    ff_width = w_gate.shape[1]
    query_end = query_width
    kv_end = query_end + 2 * HEAD_WIDTH
    z_end = kv_end + inner
    conv_end = z_end + inner + 2 * STATE_WIDTH
    step_end = conv_end + heads
    edges = (query_end, kv_end, z_end, conv_end, step_end)
    conv_width = inner + 2 * STATE_WIDTH

    shift = (deal[0, 0] // (rows // contexts) - lax.axis_index("context")) % contexts
    own_inputs = jnp.concatenate(
        [w_query, w_key, w_value, w_gate_z, w_ssm_in, w_bc, w_step], axis=1
    )
    in_shards = gather_shards(own_inputs)
    token_pieces = deal_rows(tokens, shift)
    cot_pieces = deal_rows(cotangent, shift)
    out_shards = gather_shards(jnp.concatenate([w_attn_out, w_ssm_out], axis=1))
    gate_up_shards = gather_shards(jnp.concatenate([w_gate, w_up], axis=1))
    down_shards = gather_shards(w_down)
    attn_gain = attn_norm_gain.reshape(1, D)
    ff_gain = ff_norm_gain.reshape(1, D)
    ssm_gain = ssm_norm_gain.reshape(1, inner)
    taps = jnp.concatenate([conv_ssm, conv_bc], axis=0).T
    params = jnp.pad(jnp.stack([step_bias, decay_log, skip_gain]), ((0, 5), (0, LANES - heads)))

    places = lax.axis_index("context") * rows + jnp.arange(rows, dtype=jnp.int32)
    ends = jnp.cumsum(lengths[0])
    starts = jnp.max(jnp.where(ends[None, :] <= places[:, None], ends[None, :], 0), axis=1)
    half = HEAD_WIDTH // 2
    freqs = rope_base ** (-(jnp.arange(LANES) % half).astype(f32) / half)
    angles = (places - starts).astype(f32)[:, None] * freqs[None, :]
    cosine, sine = jnp.cos(angles), jnp.sin(angles)

    x, normed, query, kv, z, conv_in, step_raw = run(
        functools.partial(project_kernel, (len(token_pieces), len(in_shards), edges)),
        [
            arr(rows, D, bf16), arr(rows, D, bf16), arr(rows, query_width, bf16),
            arr(rows, LANES, bf16), arr(rows, inner, f32), arr(rows, conv_width, bf16),
            arr(rows, LANES, f32),
        ],
        (deal, attn_gain, cosine, sine, *token_pieces, *in_shards),
        smem=(0,), flops=10**9, name="project",
    )
    halo = passed_along(conv_in[rows - 8 :], "context", 1)
    if contexts > 4:
        kv_blocks = [lax.all_gather(kv, "context", axis=0)]
    else:
        kv_blocks = [kv] + [passed_along(kv, "context", k) for k in range(1, contexts)]

    act, y_local, packed, cumulative = run(
        space_kernel,
        [
            arr(rows, conv_width, f32), arr(rows, inner, f32),
            arr(inner + 2 * GAIN_ROWS, LANES, bf16), arr(rows, LANES, f32),
        ],
        (lengths, conv_in, halo, step_raw, taps, params),
        smem=(0,), flops=10**9, name="space",
        scratch=[
            pltpu.VMEM((rows + 8, conv_width), f32), pltpu.VMEM((rows, inner), bf16),
            pltpu.VMEM((LANES, rows), f32), pltpu.VMEM((rows, rows), f32),
            pltpu.VMEM((rows, rows), f32),
        ],
    )
    near, far = relay(packed, 1)
    query_heads = query_width // HEAD_WIDTH
    per_head = jax.ShapeDtypeStruct((query_heads, rows, LANES), f32)
    attended, attended_exact, log_sum = run(
        functools.partial(attend_kernel, len(kv_blocks)),
        [arr(rows, query_width, bf16), arr(rows, query_width, f32), per_head],
        (lengths, query, *kv_blocks),
        smem=(0,), flops=10**9, name="attend",
        scratch=[pltpu.VMEM((query_heads, rows, LANES), f32)] * 3,
    )
    state, carried, ssm_y, square = run(
        gate_kernel,
        [arr(inner, LANES, bf16), arr(rows, inner, f32), arr(rows, inner, f32), arr(rows, LANES, f32)],
        (lengths, near, far, act, y_local, cumulative, z),
        smem=(0,), flops=10**8, name="gate",
    )
    square_other = swap(square, "tensor", 1)
    both, mix_part = run(
        mix_kernel,
        [arr(rows, query_width + inner, bf16), arr(rows, D, f32)],
        (attended, ssm_y, z, square, square_other, ssm_gain, *out_shards),
        flops=10**9, name="mix",
    )
    mix_other = swap(mix_part, "tensor", 1)
    mixer, normed_ff, gate, up = run(
        hidden_kernel,
        [arr(rows, D, f32), arr(rows, D, bf16), arr(rows, ff_width, f32), arr(rows, ff_width, f32)],
        (x, mix_part, mix_other, ff_gain, *gate_up_shards),
        flops=10**9, name="hidden",
    )
    (cot,) = run(
        functools.partial(place_kernel, len(cot_pieces)),
        [arr(rows, D, bf16)],
        (deal, *cot_pieces),
        smem=(0,), flops=10**6, name="place",
    )
    hidden, pair, ff_part, back = run(
        functools.partial(down_kernel, len(down_shards)),
        [
            arr(rows, ff_width, bf16), arr(rows, 2 * ff_width, bf16), arr(rows, D, f32),
            arr(rows, D, f32),
        ],
        (gate, up, cot, *gate_up_shards, *down_shards),
        flops=2 * 10**9, name="down",
    )
    back_other = swap(back, "tensor", 1)
    ff_other = swap(ff_part, "tensor", 1)
    ff_grads = run(
        ff_grad_kernel, grad_shapes(3 * ff_width), (normed_ff, pair, cot, hidden),
        flops=2 * 10**9, name="ff_grad",
    )
    grad_gate, grad_up, grad_down = reduce_grad(ff_grads, [ff_width] * 3)
    output, stats = run(
        final_kernel,
        [arr(rows, D, bf16), arr(8, LANES, f32)],
        (x, mixer, ff_part, ff_other),
        flops=10**7, name="final",
    )

    grad_resid, grad_low, grad_attended, grad_mixed, inner_sum, gain_sums = run(
        resid_back_kernel,
        [
            arr(rows, D, f32), arr(rows, D, bf16), arr(rows, query_width, bf16),
            arr(rows, inner, f32), arr(rows, LANES, f32), arr(8, D, f32),
        ],
        (back, back_other, x, mixer, cot, ff_gain, ssm_y, z, square, square_other, ssm_gain,
         *out_shards),
        flops=10**9, name="resid_back",
    )
    inner_other = swap(inner_sum, "tensor", 1)
    out_grads = run(
        weight_grad_kernel, grad_shapes(query_width + inner), (grad_low, both),
        flops=10**9, name="out_grad",
    )
    grad_attn_out, grad_ssm_out = reduce_grad(out_grads, [query_width, inner])
    out_grad, z_grad, back_packed, cmat_grad, carry_grad = run(
        gate_back_kernel,
        [
            arr(rows, inner, f32), arr(rows, inner, bf16),
            arr(inner + 2 * GAIN_ROWS, LANES, bf16), arr(rows, LANES, f32), arr(rows, LANES, f32),
        ],
        (lengths, grad_mixed, inner_sum, inner_other, square, square_other, ssm_gain, ssm_y, z,
         carried, act, cumulative, state),
        smem=(0,), flops=10**9, name="gate_back",
    )
    near, far = relay(back_packed, -1)
    if contexts > 4:
        kv_grad_shapes = [jax.ShapeDtypeStruct((contexts, rows, LANES), bf16)]
    else:
        kv_grad_shapes = [arr(rows, LANES, f32)] + [arr(rows, LANES, bf16)] * (contexts - 1)
    query_grad, *kv_grads = run(
        functools.partial(attend_back_kernel, len(kv_blocks)),
        [arr(rows, query_width, bf16), *kv_grad_shapes],
        (lengths, query, grad_attended, attended_exact, log_sum, cosine, sine, *kv_blocks),
        smem=(0,), flops=10**9, name="attend_back",
        scratch=[pltpu.VMEM((query_heads, rows, LANES), f32)] * 2,
    )
    if contexts > 4:
        kv_grads = [
            lax.psum_scatter(kv_grads[0], "context", scatter_dimension=0, tiled=False)
        ]
    else:
        kv_grads = [kv_grads[0]] + [
            passed_along(kv_grads[k], "context", -k) for k in range(1, contexts)
        ]
    scaled_grad, grad_inner = run(
        space_back_kernel,
        [arr(rows, inner, f32), arr(rows, rows, f32)],
        (lengths, out_grad, act, cumulative, step_raw, params),
        smem=(0,), flops=10**9, name="space_back",
        scratch=[
            pltpu.VMEM((rows, inner), bf16), pltpu.VMEM((LANES, rows), f32),
            pltpu.VMEM((rows, rows), f32), pltpu.VMEM((rows, rows), f32),
            pltpu.VMEM((rows, inner), bf16),
        ],
    )
    ssm_grad, bc_grad, halo_grad, halo_bc, step_grad, tap_grad, small = run(
        conv_back_kernel,
        [
            arr(rows, inner, f32), arr(rows + 8, 2 * STATE_WIDTH, f32), arr(8, conv_width, f32),
            arr(8, 2 * STATE_WIDTH, f32), arr(rows, LANES, bf16), arr(8, conv_width, f32),
            arr(8, LANES, f32),
        ],
        (lengths, near, far, out_grad, scaled_grad, grad_inner, act, y_local, step_raw, conv_in,
         halo, taps, params, state, cmat_grad, carry_grad),
        smem=(0,), flops=10**9, name="conv_back",
        scratch=[
            pltpu.VMEM((rows + 8, conv_width), f32), pltpu.VMEM((rows + 16, conv_width), f32),
        ],
    )
    bc_other = swap(bc_grad, "tensor", 1)
    halo_next = passed_along(halo_grad, "context", -1)
    cross = [
        ((c + 1) * tensors + t, c * tensors + (t ^ 1))
        for c in range(contexts - 1)
        for t in range(tensors)
    ]
    halo_bc_next = lax.ppermute(halo_bc, ("context", "tensor"), cross)
    early, late, first_part, tap_sums = run(
        functools.partial(inputs_back_kernel, (len(kv_grads), len(in_shards), edges)),
        [
            arr(rows, z_end, bf16), arr(rows, step_end - z_end, bf16), arr(rows, D, f32),
            arr(8, conv_width, f32),
        ],
        (ssm_grad, bc_grad, bc_other, halo_next, halo_bc_next, step_grad, query_grad, z_grad,
         cosine, sine, tap_grad, *kv_grads, *in_shards),
        flops=10**9, name="inputs_back",
    )
    first_other = swap(first_part, "tensor", 1)
    late_grads = run(
        weight_grad_kernel, grad_shapes(step_end - z_end), (normed, late),
        flops=10**9, name="late_grad",
    )
    early_grads = run(
        weight_grad_kernel, grad_shapes(z_end), (normed, early), flops=10**9, name="early_grad",
    )
    grad_query, grad_key, grad_value, grad_z = reduce_grad(
        early_grads, [query_width, HEAD_WIDTH, HEAD_WIDTH, inner]
    )
    grad_ssm_in, grad_bc, grad_step = reduce_grad(late_grads, [inner, 2 * STATE_WIDTH, heads])
    input_grad, sums = run(
        first_back_kernel,
        [arr(rows, D, f32), arr(8, conv_width, f32)],
        (x, grad_resid, first_part, first_other, attn_gain, gain_sums, tap_sums, small, stats),
        flops=10**7, name="first_back",
    )
    sums = sum_small(sums)
    token_count = rows * contexts * lax.axis_size("fsdp")
    rms_stats = jnp.sqrt(sums[7, LANES : LANES + 3] / (token_count * D))
    tap_sums = sums[2 : 2 + KC].T
    return (
        output,
        input_grad,
        sums[0],
        sums[1],
        grad_query,
        grad_key,
        grad_value,
        grad_attn_out,
        grad_z,
        grad_ssm_in,
        grad_bc,
        grad_step,
        grad_ssm_out,
        tap_sums[:inner],
        tap_sums[inner:],
        sums[6, inner : inner + heads],
        sums[6, inner + LANES : inner + LANES + heads],
        sums[7, :heads],
        sums[6, :inner],
        grad_gate,
        grad_up,
        grad_down,
        rms_stats,
    )


def solution(mesh):
    rows = P(("fsdp", "context"), None)
    weight = P("fsdp", "tensor")
    return jax.shard_map(
        per_device,
        mesh=mesh,
        in_specs=(
            rows, P("fsdp", None), P("fsdp", "context"), P(), P(), weight, weight, weight, weight,
            weight, weight, P("fsdp", None), weight, weight, P("tensor", None), P(), P("tensor"),
            P("tensor"), P("tensor"), P("tensor"), weight, weight, weight, rows,
        ),
        out_specs=(
            rows, rows, P(), P(), weight, weight, weight, weight, weight, weight, P("fsdp", None),
            weight, weight, P("tensor", None), P(), P("tensor"), P("tensor"), P("tensor"),
            P("tensor"), weight, weight, weight, P(),
        ),
        check_vma=False,
    )
```
